256 devices in a mesh: row: 8 (over x_hi, y), col: 32 (over z, x_lo, core).
Axes of the slice: x: 4 (x_hi: 2, x_lo: 2; x = x_hi * 2 + x_lo), y: 4, z: 8, core: 2. Of those that a mesh axis runs over, the one named last changes fastest.
Arguments:
- region_inverse: float32 [4096, 4096], P('row', 'col'), may hold values from -6 to 6
- factor_cols: float32 [3, 4096, 512], P(None, 'row'), may hold values from -0.09375 to 0.09375
- parent_factor: float32 [2, 512, 512], P(None, 'col'), may hold values from -0.25 to 0.25
- diag_inverse: float32 [3, 512, 512], P(None, 'col'), may hold values from -6 to 6
- listed: int32 [3, 8], replicated, may hold values from 0 to 1, as said below
Outputs:
- col_blocks: float32 [3, 4096, 512], P(None, ('row', 'col'))
- diag_blocks: float32 [3, 512, 512], P(None, 'col')
- parent_rows: float32 [2, 512, 512], P(None, 'col')
The draws below stay inside these ranges and needn't reach their ends.
Inputs may be any that keep to these rules, and one draw needn't show every extreme that they name: listed[0] has exactly 6 ones; listed[1] and listed[2] have exactly 4 ones each, all at blocks that listed[0] also lists.
All inputs are finite; a program needn't handle non-finite values.
Results may differ from the reference program's by a relative error of at most 0.0001.
Values sent between devices are 32-bit elements; how exact they have to be, the bound alone decides.
A program may use at most 64 MiB of HBM per device.

```python
import jax
import jax.numpy as jnp
from jax import lax

B = 512
NB = 8
R = 4096
LP = 6
LC = 4


def draw_listed(key, part):
    first = jax.random.permutation(jax.random.fold_in(key, 11), NB)
    parent = jnp.zeros((NB,), jnp.int32).at[first[:LP]].set(1)
    result_rows = [parent]
    for member in range(2):
        order = jax.random.permutation(jax.random.fold_in(key, 21 + member), LP)
        picked = first[order[:LC]]
        result_rows.append(jnp.zeros((NB,), jnp.int32).at[picked].set(1))
    return jnp.stack(result_rows)


def raised(values, stream_key, source, target, shards_of, factor):
    def block_of(dim):
        return (jnp.arange(values.shape[dim]) // (values.shape[dim] // shards_of)).reshape((-1,) + (1,) * (values.ndim - 1 - dim))

    first = jax.random.permutation(stream_key, shards_of)[block_of(target)]
    other_side = (block_of(target) + shards_of // 2) % shards_of
    return jnp.where((block_of(source) == first) | (block_of(source) == other_side), factor * values, values)


def block_levels(key, dims, split, smallest, largest):
    factor_of, own = 1.0, jax.random.fold_in(key, 6)
    for position, parts in split:
        draws = jnp.exp(jax.random.uniform(jax.random.fold_in(own, position), (parts,), jnp.float32, smallest / len(split), largest / len(split)))
        factor_of = factor_of * jnp.repeat(draws, dims[position] // parts).reshape([-1 if axis == position else 1 for axis in range(len(dims))])
    return factor_of


def scatter_about(key, dims, deviation, most, split=(), dtype=jnp.bfloat16):
    result = jax.random.normal(key, dims, jnp.float32) * deviation
    if len(split) > 0:
        result = block_levels(key, dims, split, -0.22, 0.18) * result
    return jnp.clip(result, min=-most, max=most).astype(dtype)


def gaussian_with(stream_key, dims, width, limit, pieces, heavy, kind=jnp.bfloat16):
    drawn = width * jax.random.normal(stream_key, dims, jnp.float32)
    if pieces:
        drawn = drawn * block_levels(stream_key, dims, pieces, -0.22, 0.18)
    return jnp.clip(raised(drawn, jax.random.fold_in(stream_key, 3), *heavy), -limit, limit).astype(kind)


def setup_inputs(seed: int = 0) -> dict:
    key_list = jax.random.split(jax.random.key(seed), 6)
    return {
        "region_inverse": gaussian_with(key_list[0], (R, R), 1.0, 6.0, ((0, 8), (1, 32)), (1, 0, 32, 2.75), jnp.float32),
        "factor_cols": scatter_about(key_list[1], (3, R, B), R ** -0.5, 0.09375, ((1, 8),), jnp.float32),
        "parent_factor": scatter_about(key_list[2], (2, B, B), B ** -0.5, 0.25, ((1, 32),), jnp.float32),
        "diag_inverse": scatter_about(key_list[3], (3, B, B), 1.0, 6.0, ((1, 32),), jnp.float32),
        "listed": draw_listed(jax.random.fold_in(key_list[5], 71), 0),
    }


def product(left, right):
    return jnp.dot(left, right, precision=lax.Precision.HIGHEST, preferred_element_type=jnp.float32)


def reference(region_inverse, factor_cols, parent_factor, diag_inverse, listed):
    weights = listed.astype(jnp.float32)
    masks = [jnp.repeat(weights[member], B) for member in range(3)]
    factors = [factor_cols[member] * masks[member][:, None] for member in range(3)]
    parent_col = -product(region_inverse, factors[0]) * masks[0][:, None]
    parent_diag = diag_inverse[0] - product(factors[0].T, parent_col)
    col_list = [parent_col]
    diag_list = [parent_diag]
    upper_list = []
    for member in (1, 2):
        link = parent_factor[member - 1]
        column = -(product(region_inverse, factors[member]) + product(parent_col, link)) * masks[member][:, None]
        upper = -(product(parent_col.T, factors[member]) + product(parent_diag, link))
        diagonal = diag_inverse[member] - product(factors[member].T, column) - product(link.T, upper)
        col_list.append(column)
        diag_list.append(diagonal)
        upper_list.append(upper)
    return jnp.stack(col_list), jnp.stack(diag_list), jnp.stack(upper_list)
```

```python
import functools

import jax
import jax.numpy as jnp
from jax import lax
from jax.experimental import pallas as pl
from jax.experimental.pallas import tpu as pltpu
from jax.sharding import PartitionSpec as P

MESH = pl.DeviceIdType.MESH
HIGH = lax.Precision.HIGHEST

S_A, S_FS, S_FA, S_G, S_GN, S_D, S_RB, S_Y0, S_YO, S_YU, S_TR, S_ZM, S_ZB, S_WM, S_WB, S_UO, S_GZ, S_ZO = range(0, 54, 3)
N_SEM = 54


def mm(a, b):
    return jnp.dot(a, b, precision=HIGH, preferred_element_type=jnp.float32)


def mm_t(a, b):
    return lax.dot_general(
        a, b, (((0,), (0,)), ((), ())), precision=HIGH, preferred_element_type=jnp.float32
    )


def kernel(
    R, C, W, planes,
    a_ref, f_ref, g_ref, d_ref, listed_ref,
    col_ref, diag_ref, par_ref,
    abuf, fb, pb, rb, gc, gn, db, y0n, yc, yo, yu, tp, tpw, tr, trw, ts, tsw,
    zm, zb, wm, wb, eb, uo, ge, gz, zp, zo, send, recv, sendx,
):
    Q = C // R
    NQ, HZ, GC = W // Q, W // R, W // C
    SP = HZ // R
    HW = NQ // HZ
    r = lax.axis_index("row")
    c = lax.axis_index("col")
    z = c // Q
    q = c % Q

    def flip(row, place):
        return 2 * ((place // 2 + row // (R // 2)) % 2) + place % 2

    n = flip(r, q)
    partner = (z + R // 2) % R
    n_cols = pl.ds(pl.multiple_of(n * NQ, NQ), NQ)
    my_rows = pl.ds(pl.multiple_of(z * HZ, HZ), HZ)

    def push(src, dst, s, row, col, k=0):
        pltpu.make_async_remote_copy(
            src_ref=src, dst_ref=dst, send_sem=send.at[s + k], recv_sem=recv.at[s + k],
            device_id=(row, col), device_id_type=MESH,
        ).start()

    def arrived(view, s, k=0):
        pltpu.make_async_copy(view, view, recv.at[s + k]).wait()

    def sent(view, s, k=0):
        pltpu.make_async_copy(view, view, send.at[s + k]).wait()

    def weight(member, block):
        return listed_ref[member, block].astype(jnp.float32)

    barrier = pltpu.get_barrier_semaphore()

    @pl.loop(1, C)
    def _(k):
        pl.semaphore_signal(barrier, inc=1, device_id=(r, (c + k) % C), device_id_type=MESH)

    @pl.loop(1, R)
    def _(k):
        for place in range(Q):
            pl.semaphore_signal(
                barrier, inc=1, device_id=((r + k) % R, z * Q + place), device_id_type=MESH
            )

    pl.semaphore_wait(barrier, C - 1 + (R - 1) * Q)

    def piece(i):
        return pl.ds(pl.multiple_of(i * HZ, HZ), HZ)

    @pl.when(r == z)
    def _():
        for j in range(3):
            for k in range(1, R):
                i = (z + k) % R
                push(
                    f_ref.at[j, piece(i), n_cols], fb.at[j, piece(i)], S_FS, i, z * Q + flip(i, n), j
                )
            push(
                f_ref.at[j, piece(z), n_cols], fb.at[j, piece(z)], S_FS,
                partner, z * Q + flip(partner, n), j,
            )

    a_cols = pl.ds(pl.multiple_of(q * NQ, NQ), NQ)
    for k in range(1, Q):
        push(a_ref, abuf.at[:, a_cols], S_A, r, z * Q + (q + k) % Q)

    g_rows = pl.ds(pl.multiple_of(c * GC, GC), GC)
    n_rows = pl.ds(pl.multiple_of(q * GC, GC), GC)

    @pl.loop(1, C)
    def _(k):
        other = (c + k) % C
        share = flip(r, other % Q)
        push(
            g_ref.at[:, :, pl.ds(pl.multiple_of(share * NQ, NQ), NQ)], gc.at[:, g_rows], S_G, r, other
        )

    for k in range(1, Q):
        push(g_ref, gn.at[:, n_rows], S_GN, r, z * Q + (q + k) % Q)
        push(d_ref.at[0], db.at[n_rows], S_D, r, z * Q + (q + k) % Q)

    abuf[:, a_cols] = a_ref[...]
    gc[:, g_rows] = g_ref[:, :, n_cols]
    gn[:, n_rows] = g_ref[...]
    db[n_rows] = d_ref[0]

    @pl.when(r == z)
    def _():
        for j in range(3):
            fb[j] = f_ref[j, :, n_cols]

    @pl.when(r != z)
    def _():
        for j in range(3):
            @pl.when(r == partner)
            def _():
                arrived(fb.at[j, : 2 * HZ], S_FS, j)

            @pl.when(r != partner)
            def _():
                arrived(fb.at[j, :HZ], S_FS, j)

            for k in range(1, R):
                i = (r + k) % R

                @pl.when(i != z)
                def _():
                    push(fb.at[j, piece(r)], fb.at[j, piece(r)], S_FA, i, z * Q + flip(i, n), j)

                    @pl.when(r == partner)
                    def _():
                        pltpu.make_async_remote_copy(
                            src_ref=fb.at[j, piece(z)], dst_ref=fb.at[j, piece(z)],
                            send_sem=sendx.at[0], recv_sem=recv.at[S_FA + j],
                            device_id=(i, z * Q + flip(i, n)), device_id_type=MESH,
                        ).start()

    arrived(abuf.at[:, : (Q - 1) * NQ], S_A)

    for j in range(3):
        @pl.when((r != z) & (r != partner))
        def _():
            arrived(fb.at[j, : (R - 1) * HZ], S_FA, j)

        @pl.when(r == partner)
        def _():
            arrived(fb.at[j, : (R - 2) * HZ], S_FA, j)

        pb[j] = mm(abuf[...], fb[j]) * weight(j, z)
        for k in range(1, R):
            other = (z + k) % R
            push(
                pb.at[j, piece(other)], rb.at[j, R - 1 - k], S_RB, r, other * Q + q, j
            )

    def summed(j):
        arrived(rb.at[j], S_RB, j)
        total = pb[j, my_rows]
        for k in range(R - 1):
            total = total + rb[j, k]
        return total

    def to_unit(j, plane):
        @pl.when(z != plane)
        def _():
            push(yc.at[j], yu.at[my_rows], S_YU, r, plane * Q + q, j)

        @pl.when(z == plane)
        def _():
            yu[my_rows] = yc[j]

    yc[0] = -weight(0, r) * summed(0)
    for k in range(1, Q):
        push(yc.at[0], y0n.at[:, n_cols], S_Y0, r, z * Q + (q + k) % Q)
    for plane in planes[:3]:
        to_unit(0, plane)
    y0n[:, n_cols] = yc[0]
    arrived(y0n.at[:, : (Q - 1) * NQ], S_Y0)
    col_ref[0] = y0n[n_rows]
    arrived(gc.at[:, : (C - 1) * GC], S_G)

    for j in (1, 2):
        cross = mm(y0n[...], gc[j - 1])
        yc[j] = -weight(j, r) * (summed(j) + cross)
        to_unit(j, planes[2 + j])
        for k in range(1, Q):
            other = (q + k) % Q
            push(
                yc.at[j, pl.ds(pl.multiple_of(other * GC, GC), GC)], yo.at[j - 1, :, n_cols],
                S_YO, r, z * Q + other,
            )
        yo[j - 1, :, n_cols] = yc[j, n_rows]

    def rows_sum(unit, member, source):
        @pl.when(z == planes[unit])
        def _():
            arrived(yu.at[: (R - 1) * HZ], S_YU, source)
            if unit in (1, 2):
                tpw[...] = (mm_t(yu[...], f_ref[member]) * weight(member, r)).reshape(HW, R, SP, W)
                for k in range(1, R):
                    i = (r + k) % R
                    push(tpw.at[:, i], trw.at[R - 1 - k], S_TR, i, z * Q + flip(i, n))
            else:
                tp[...] = mm_t(f_ref[member], yu[...]).reshape(R, R, SP, NQ)
                for k in range(1, R):
                    i = (r + k) % R
                    push(tp.at[:, i], tr.at[R - 1 - k], S_TR, i, z * Q + flip(i, n))

    rows_sum(0, 0, 0)
    rows_sum(1, 1, 0)
    rows_sum(2, 2, 0)
    rows_sum(3, 1, 1)
    rows_sum(4, 2, 2)

    def spread(unit, place):
        @pl.when(z == planes[unit])
        def _():
            if unit in (1, 2):
                arrived(trw, S_TR)
                total = tpw[:, r]
                for k in range(R - 1):
                    total = total + trw[k]
                tsw[...] = total
                for h in range(HW):
                    dest = n * HW + h

                    @pl.when(dest != z)
                    def _():
                        push(tsw.at[h], wm.at[unit - 1], S_WM, r, dest * Q + q, unit - 1)

                    @pl.when(dest == z)
                    def _():
                        wm[unit - 1] = tsw[h]
            else:
                arrived(tr, S_TR)
                total = tp[:, r]
                for k in range(R - 1):
                    total = total + tr[k]
                ts[...] = total
                for k in range(1, R):
                    dest = (z + k) % R
                    push(ts.at[dest], zm.at[place], S_ZM, r, dest * Q + q, place)
                zm[place] = ts[z]

    spread(0, 0)
    spread(1, 0)
    spread(2, 0)
    spread(3, 1)
    spread(4, 2)

    s_rows = pl.ds(pl.multiple_of(r * SP, SP), SP)
    flat = r * Q + q

    @pl.when(z != planes[0])
    def _():
        arrived(zm.at[0], S_ZM, 0)

    @pl.loop(1, C)
    def _(k):
        other = (flat + k) % C
        push(zm.at[0], zb.at[s_rows, n_cols], S_ZB, other // Q, z * Q + other % Q)

    zb[s_rows, n_cols] = zm[0]

    holds_w = z // HW == n

    @pl.when(holds_w)
    def _():
        for child in range(2):
            @pl.when(z != planes[1 + child])
            def _():
                arrived(wm.at[child], S_WM, child)

            @pl.loop(1, C)
            def _(k):
                other = (flat + k) % C
                share = flip(other // Q, other % Q)
                push(
                    wm.at[child, :, pl.ds(pl.multiple_of(share * NQ, NQ), NQ)],
                    wb.at[child, s_rows], S_WB, other // Q, z * Q + other % Q, child,
                )

            wb[child, s_rows] = wm[child, :, n_cols]

    arrived(db.at[: (Q - 1) * GC], S_D)
    arrived(gn.at[:, : (Q - 1) * GC], S_GN)
    arrived(fb.at[0, : (C - 1) * SP], S_ZB)
    zb[...] = db[...] - zb[...]
    diag_ref[0] = zb[n_rows]
    for child in range(2):
        @pl.when(holds_w)
        def _():
            arrived(wb.at[child, : (R - 1) * SP], S_WB, child)

        @pl.when(jnp.logical_not(holds_w))
        def _():
            arrived(wb.at[child], S_WB, child)

        eb[child] = wb[child] + mm(zb[...], gc[child])
        ge[child] = mm_t(gn[child], eb[child]).reshape(R, R, SP, NQ)
        for k in range(1, R):
            dest = (z + k) % R
            push(ge.at[child, dest, r], gz.at[child, R - 1 - k], S_GZ, r, dest * Q + q, child)
        for k in range(1, Q):
            other = (q + k) % Q
            push(
                eb.at[child, pl.ds(pl.multiple_of(other * GC, GC), GC)], uo.at[child, :, n_cols],
                S_UO, r, z * Q + other,
            )
        uo[child, :, n_cols] = eb[child, n_rows]

    o_rows = pl.ds(pl.multiple_of(r % (R // Q) * SP, SP), SP)
    o_place = r // (R // Q)
    for child in range(2):
        @pl.when(z != planes[3 + child])
        def _():
            arrived(zm.at[1 + child], S_ZM, 1 + child)

        arrived(gz.at[child], S_GZ, child)
        total = ge[child, z, r] - zm[1 + child]
        for k in range(R - 1):
            total = total + gz[child, k]
        zp[child] = total
        for k in range(1, R):
            push(
                zp.at[child], zo.at[child, o_rows, n_cols], S_ZO, (r + k) % R, z * Q + o_place, child
            )

        @pl.when(q == o_place)
        def _():
            zo[child, o_rows, n_cols] = zp[child]

        @pl.when(q != o_place)
        def _():
            push(zp.at[child], zo.at[child, o_rows, n_cols], S_ZO, r, z * Q + o_place, child)

    arrived(yo.at[:, :, : (Q - 1) * NQ], S_YO)
    col_ref[1:3] = yo[...]
    arrived(uo.at[:, :, : (Q - 1) * NQ], S_UO)
    par_ref[...] = -uo[...]
    for child in range(2):
        @pl.when(q == o_place)
        def _():
            arrived(rb.at[child, 0, : (R - 1) * SP], S_ZO, child)

        @pl.when(q != o_place)
        def _():
            arrived(rb.at[child, 0, : R * SP], S_ZO, child)

        diag_ref[1 + child] = d_ref[1 + child] + zo[child]

    sent(abuf.at[:, : (Q - 1) * NQ], S_A)
    sent(gc.at[:, : (C - 1) * GC], S_G)
    sent(gn.at[:, : (Q - 1) * GC], S_GN)
    sent(db.at[: (Q - 1) * GC], S_D)
    sent(y0n.at[:, : (Q - 1) * NQ], S_Y0)
    sent(yo.at[:, :, : (Q - 1) * NQ], S_YO)
    sent(uo.at[:, :, : (Q - 1) * NQ], S_UO)
    sent(fb.at[0, : (C - 1) * SP], S_ZB)
    for j in range(3):
        @pl.when(r == z)
        def _():
            sent(fb.at[j], S_FS, j)

        @pl.when(r != z)
        def _():
            sent(fb.at[j, : (R - 2) * HZ], S_FA, j)

        sent(rb.at[j], S_RB, j)

    @pl.when(r == partner)
    def _():
        pltpu.make_async_copy(
            fb.at[:, : (R - 2) * HZ], fb.at[:, : (R - 2) * HZ], sendx.at[0]
        ).wait()

    for j in range(3):
        targets = planes[:3] if j == 0 else planes[2 + j : 3 + j]
        inside = functools.reduce(jnp.logical_or, [z == plane for plane in targets])

        @pl.when(inside)
        def _():
            if len(targets) > 1:
                sent(yu.at[: (len(targets) - 1) * HZ], S_YU, j)

        @pl.when(jnp.logical_not(inside))
        def _():
            sent(yu.at[: len(targets) * HZ], S_YU, j)

    for unit in range(5):
        @pl.when(z == planes[unit])
        def _():
            if unit in (1, 2):
                sent(trw, S_TR)

                @pl.when(z // HW == n)
                def _():
                    if HW > 1:
                        sent(tsw.at[: HW - 1], S_WM, unit - 1)

                @pl.when(z // HW != n)
                def _():
                    sent(tsw, S_WM, unit - 1)
            else:
                place = (0, None, None, 1, 2)[unit]
                sent(tr, S_TR)
                sent(ts.at[: R - 1], S_ZM, place)

    for child in range(2):
        @pl.when(holds_w)
        def _():
            sent(fb.at[0, : (C - 1) * SP], S_WB, child)

        sent(gz.at[child], S_GZ, child)

        @pl.when(q == o_place)
        def _():
            sent(rb.at[child, 0, : (R - 1) * SP], S_ZO, child)

        @pl.when(q != o_place)
        def _():
            sent(rb.at[child, 0, : R * SP], S_ZO, child)


def shards(region_inverse, factor_cols, parent_factor, diag_inverse, listed):
    R = lax.axis_size("row")
    C = lax.axis_size("col")
    W = factor_cols.shape[2]
    Q = C // R
    NQ, HZ, GC = W // Q, W // R, W // C
    SP = HZ // R
    HW = NQ // HZ
    planes = (0, 2, 5, 3, 7)
    f32 = jnp.float32
    vmem = pl.BlockSpec(memory_space=pltpu.VMEM)
    smem = pl.BlockSpec(memory_space=pltpu.SMEM)
    scratch = [
        (W, W), (3, W, NQ), (3, W, NQ), (3, R - 1, HZ, NQ), (2, W, NQ), (2, HZ, W), (HZ, W),
        (HZ, W), (3, HZ, NQ), (2, GC, W), (W, NQ),
        (R, R, SP, NQ), (HW, R, SP, W), (R - 1, R, SP, NQ), (R - 1, HW, SP, W),
        (R, SP, NQ), (HW, SP, W),
        (3, SP, NQ), (HZ, W), (2, SP, W), (2, HZ, NQ), (2, HZ, NQ), (2, GC, W),
        (2, R, R, SP, NQ), (2, R - 1, SP, NQ), (2, SP, NQ), (2, GC, W),
    ]
    return pl.pallas_call(
        functools.partial(kernel, R, C, W, planes),
        out_shape=(
            jax.ShapeDtypeStruct((3, GC, W), f32),
            jax.ShapeDtypeStruct((3, GC, W), f32),
            jax.ShapeDtypeStruct((2, GC, W), f32),
        ),
        in_specs=[vmem, vmem, vmem, vmem, smem],
        out_specs=(vmem, vmem, vmem),
        scratch_shapes=[pltpu.VMEM(shape, f32) for shape in scratch]
        + [
            pltpu.SemaphoreType.DMA((N_SEM,)),
            pltpu.SemaphoreType.DMA((N_SEM,)),
            pltpu.SemaphoreType.DMA((1,)),
        ],
        compiler_params=pltpu.CompilerParams(collective_id=0, has_side_effects=True),
    )(region_inverse, factor_cols, parent_factor, diag_inverse, listed)


def solution(mesh):
    in_specs = (
        P("row", "col"),
        P(None, "row", None),
        P(None, "col", None),
        P(None, "col", None),
        P(),
    )
    out_specs = (P(None, ("row", "col"), None), P(None, "col", None), P(None, "col", None))
    return jax.shard_map(shards, mesh=mesh, in_specs=in_specs, out_specs=out_specs, check_vma=False)
```

```python
import functools

import jax
import jax.numpy as jnp
from jax import lax
from jax.experimental import pallas as pl
from jax.experimental.pallas import tpu as pltpu
from jax.sharding import PartitionSpec as P

MESH = pl.DeviceIdType.MESH
HIGH = lax.Precision.HIGHEST

SIZES = dict(
    A=3, FS=3, FA=3, GN=1, D=1, GP=4, GM=3, X=3, RB=3, Y0=1, YO=1, YU=3, TR=1, ZM=3, ZB=1, WM=2, WB=2,
    UO=1, GZ=2, ZO=2, FX=1, FB=3, FV=1,
)
BASE = {}
N_SEM = 0
for _name, _size in SIZES.items():
    BASE[_name] = N_SEM
    N_SEM += _size

OFFSET = {1: 0, 3: 0, 4: 0, 2: -1, 7: -1, 5: 1, 6: 1}


def mm(a, b):
    return jnp.dot(a, b, precision=HIGH, preferred_element_type=jnp.float32)


def mm_t(a, b):
    return lax.dot_general(
        a, b, (((0,), (0,)), ((), ())), precision=HIGH, preferred_element_type=jnp.float32
    )


def kernel(
    R, C, W, planes,
    a_ref, f_ref, g_ref, d_ref, listed_ref,
    out_ref,
    abuf, fb, fv, pb, xb, rl, rb, gc, gn, db, y0n, yc, xc, yo, yu, tp, tpw, tr, trw, ts, tsw,
    zm, zb, wm, wb, eb, uo, ge, gz, zp, zo, send, recv,
):
    Q = C // R
    NQ, HZ, GC = W // Q, W // R, W // C
    SP = HZ // R
    HW = NQ // HZ
    HR = R // 2
    r = lax.axis_index("row")
    c = lax.axis_index("col")
    z = c // Q
    q = c % Q

    def flip(row, place):
        return 2 * ((place // 2 + row // HR) % 2) + place % 2

    def at(row, k):
        return (row // HR + k // HR) % 2 * HR + (row % HR + k % HR) % HR

    n = flip(r, q)
    partner = at(z, HR)
    core = q % 2
    sibling = q + 1 - 2 * core
    across = (q + 2) % Q
    n_cols = pl.ds(pl.multiple_of(n * NQ, NQ), NQ)

    def piece(i):
        return pl.ds(pl.multiple_of(i * HZ, HZ), HZ)

    my_rows = piece(z)

    def push(src, dst, s, row, col, k=0):
        s = BASE[s] + k
        pltpu.make_async_remote_copy(
            src_ref=src, dst_ref=dst, send_sem=send.at[s], recv_sem=recv.at[s],
            device_id=(row, col), device_id_type=MESH,
        ).start()

    def arrived(view, s, k=0):
        pltpu.make_async_copy(view, view, recv.at[BASE[s] + k]).wait()

    def sent(view, s, k=0):
        pltpu.make_async_copy(view, view, send.at[BASE[s] + k]).wait()

    def weight(member, block):
        return listed_ref[member, block].astype(jnp.float32)

    barrier = pltpu.get_barrier_semaphore()

    def greet(row, col):
        pl.semaphore_signal(barrier, inc=1, device_id=(row, col), device_id_type=MESH)

    for k in range(1, R):
        i = at(r, k)
        greet(i, z * Q + flip(i, n))
    for k in range(1, R):
        greet(r, (z + k) % R * Q + q)
    for k in range(1, Q):
        greet(r, z * Q + (q + k) % Q)
    for k, offset in OFFSET.items():
        if offset:
            @pl.when(at(z, k) == r)
            def _():
                greet(z, (z + offset) % R * Q + flip(z, n))

    near = z == r
    above = z == (r + 1) % R
    below = (z + 1) % R == r
    peers = 2 * (R - 1) + Q - 1

    @pl.when(above | below)
    def _():
        pl.semaphore_wait(barrier, peers + 2)

    @pl.when(jnp.logical_not(above | below))
    def _():
        pl.semaphore_wait(barrier, peers)

    for offset, here in ((0, near), (1, above), (-1, below)):
        @pl.when(here)
        def _():
            for j in range(3):
                for k, source in OFFSET.items():
                    if source == offset:
                        i = at(r, k)
                        push(
                            f_ref.at[j, piece(i), n_cols], fb.at[j, piece(i)], "FS",
                            i, r * Q + flip(i, n), j,
                        )
                if offset == 0:
                    push(
                        f_ref.at[j, piece(z), n_cols], fb.at[j, piece(z)], "FS",
                        partner, z * Q + flip(partner, n), j,
                    )

    a_cols = pl.ds(pl.multiple_of(q * NQ, NQ), NQ)
    x_cols = pl.ds(pl.multiple_of(across * NQ, NQ), NQ)
    push(a_ref, abuf.at[:, a_cols], "A", r, z * Q + across, 1)
    push(a_ref, abuf.at[:, a_cols], "A", r, z * Q + sibling, 0)
    keep = pltpu.make_async_copy(f_ref, fv, recv.at[BASE["FV"]])

    @pl.when(near)
    def _():
        for j in range(3):
            pltpu.make_async_copy(f_ref.at[j, :, n_cols], fb.at[j], recv.at[BASE["FB"] + j]).start()

    keep.start()

    n_rows = pl.ds(pl.multiple_of(q * GC, GC), GC)
    for k in range(1, Q):
        push(g_ref, gn.at[:, n_rows], "GN", r, z * Q + (q + k) % Q)
        push(d_ref.at[0], db.at[n_rows], "D", r, z * Q + (q + k) % Q)
    abuf[:, a_cols] = a_ref[...]
    gn[:, n_rows] = g_ref[...]
    db[n_rows] = d_ref[0]

    def forward(j):
        @pl.when(r != z)
        def _():
            @pl.when(r == partner)
            def _():
                arrived(fb.at[j, : 2 * HZ], "FS", j)

            @pl.when(r != partner)
            def _():
                arrived(fb.at[j, :HZ], "FS", j)

            for k in range(1, R):
                i = at(r, k)

                @pl.when(i != z)
                def _():
                    push(fb.at[j, piece(r)], fb.at[j, piece(r)], "FA", i, z * Q + flip(i, n), j)

                    @pl.when(r == partner)
                    def _():
                        pltpu.make_async_remote_copy(
                            src_ref=fb.at[j, piece(z)], dst_ref=fb.at[j, piece(z)],
                            send_sem=send.at[BASE["FX"]], recv_sem=recv.at[BASE["FA"] + j],
                            device_id=(i, z * Q + flip(i, n)), device_id_type=MESH,
                        ).start()

    def g_step(k):
        if k == 0:
            arrived(gn.at[:, : (Q - 1) * GC], "GN")
            gc[:, my_rows] = gn[:, :, n_cols]
        up = gn.at[:, :, n_cols] if k == 0 else gc.at[:, piece((z - k) % R)]
        down = gn.at[:, :, n_cols] if k == 0 else gc.at[:, piece((z + k) % R)]
        if k:
            arrived(up, "GP", k - 1)
        push(up, gc.at[:, piece((z - k) % R)], "GP", r, (z + 1) % R * Q + q, k)
        if k < R - 1 - HR:
            if k:
                arrived(down, "GM", k - 1)
            push(down, gc.at[:, piece((z + k) % R)], "GM", r, (z - 1) % R * Q + q, k)

    s = 1 - 2 * core

    def along(k):
        return (z + s * k) % R

    def product(j):
        @pl.when(r == z)
        def _():
            pltpu.make_async_copy(fb.at[j], fb.at[j], recv.at[BASE["FB"] + j]).wait()

        @pl.when((r != z) & (r != partner))
        def _():
            arrived(fb.at[j, : (R - 1) * HZ], "FA", j)

        @pl.when(r == partner)
        def _():
            arrived(fb.at[j, : (R - 2) * HZ], "FA", j)

        pb[j] = mm(abuf[...], fb[j]) * weight(j, z)

        def part(k):
            return pb.at[j, piece(along(k))]

        push(part(4), xb.at[j, 0], "X", r, along(2) * Q + q, j)
        push(part(3), xb.at[j, 1], "X", r, along(1) * Q + q, j)
        push(part(-3), xb.at[j, 2], "X", r, along(-1) * Q + q, j)
        push(part(1), rb.at[j, 0], "RB", r, along(1) * Q + q, j)
        push(part(-1), rb.at[j, 1], "RB", r, along(-1) * Q + q, j)

    def relay(j):
        arrived(xb.at[j], "X", j)
        rl[j, 0] = pb[j, piece(along(2))] + xb[j, 0] + xb[j, 1]
        rl[j, 1] = pb[j, piece(along(-2))] + xb[j, 2]
        push(rl.at[j, 0], rb.at[j, 2], "RB", r, along(2) * Q + q, j)
        push(rl.at[j, 1], rb.at[j, 3], "RB", r, along(-2) * Q + q, j)

    forward(0)
    forward(1)
    arrived(abuf.at[:, x_cols], "A", 1)
    push(abuf.at[:, x_cols], abuf.at[:, x_cols], "A", r, z * Q + sibling, 2)
    forward(2)
    g_step(0)
    arrived(abuf.at[:, a_cols], "A", 0)
    arrived(abuf.at[:, a_cols], "A", 2)
    product(0)
    g_step(1)
    product(1)
    relay(0)
    product(2)
    relay(1)
    g_step(2)
    relay(2)
    g_step(3)

    def summed(j):
        arrived(rb.at[j], "RB", j)
        return ((pb[j, my_rows] + rb[j, 0]) + (rb[j, 1] + rb[j, 2])) + rb[j, 3]

    def to_unit(j, plane):
        @pl.when(z != plane)
        def _():
            push(yc.at[j], yu.at[my_rows], "YU", r, plane * Q + q, j)

        @pl.when(z == plane)
        def _():
            yu[my_rows] = yc[j]

    yc[0] = -weight(0, r) * summed(0)
    for k in range(1, Q):
        push(yc.at[0], y0n.at[:, n_cols], "Y0", r, z * Q + (q + k) % Q)
    for plane in planes[:3]:
        to_unit(0, plane)
    y0n[:, n_cols] = yc[0]
    arrived(y0n.at[:, : (Q - 1) * NQ], "Y0")
    out_ref[0] = y0n[n_rows]
    arrived(gc.at[:, piece((z - HR) % R)], "GP", HR - 1)
    arrived(gc.at[:, piece((z + HR - 1) % R)], "GM", HR - 2)
    for j in (1, 2):
        xc[j - 1] = mm(y0n[...], gc[j - 1])

    def child_columns(j):
        yc[j] = -weight(j, r) * (summed(j) + xc[j - 1])
        to_unit(j, planes[2 + j])
        for k in range(1, Q):
            other = (q + k) % Q
            push(
                yc.at[j, pl.ds(pl.multiple_of(other * GC, GC), GC)], yo.at[j - 1, :, n_cols],
                "YO", r, z * Q + other,
            )
        yo[j - 1, :, n_cols] = yc[j, n_rows]

    def rows_sum(unit, member, source):
        @pl.when(z == planes[unit])
        def _():
            arrived(yu.at[: (R - 1) * HZ], "YU", source)
            if unit in (1, 2):
                tpw[...] = (mm_t(yu[...], fv[member]) * weight(member, r)).reshape(HW, R, SP, W)
                for k in range(1, R):
                    i = (r + k) % R
                    push(tpw.at[:, i], trw.at[R - 1 - k], "TR", i, z * Q + flip(i, n))
            else:
                tp[...] = mm_t(fv[member], yu[...]).reshape(R, R, SP, NQ)
                for k in range(1, R):
                    i = (r + k) % R
                    push(tp.at[:, i], tr.at[R - 1 - k], "TR", i, z * Q + flip(i, n))


    def spread(unit, place):
        @pl.when(z == planes[unit])
        def _():
            if unit in (1, 2):
                arrived(trw, "TR")
                total = tpw[:, r]
                for k in range(R - 1):
                    total = total + trw[k]
                tsw[...] = total
                for h in range(HW):
                    dest = n * HW + h

                    @pl.when(dest != z)
                    def _():
                        push(tsw.at[h], wm.at[unit - 1], "WM", r, dest * Q + q, unit - 1)

                    @pl.when(dest == z)
                    def _():
                        wm[unit - 1] = tsw[h]
            else:
                arrived(tr, "TR")
                total = tp[:, r]
                for k in range(R - 1):
                    total = total + tr[k]
                ts[...] = total
                for k in range(1, R):
                    dest = (z + k) % R
                    push(ts.at[dest], zm.at[place], "ZM", r, dest * Q + q, place)
                zm[place] = ts[z]

    keep.wait()
    rows_sum(0, 0, 0)
    rows_sum(1, 1, 0)
    rows_sum(2, 2, 0)
    child_columns(1)
    spread(0, 0)
    spread(1, 0)
    spread(2, 0)
    child_columns(2)

    s_rows = pl.ds(pl.multiple_of(r * SP, SP), SP)
    flat = r * Q + q

    @pl.when(z != planes[0])
    def _():
        arrived(zm.at[0], "ZM", 0)

    @pl.loop(1, C)
    def _(k):
        other = (flat + k) % C
        push(zm.at[0], zb.at[s_rows, n_cols], "ZB", other // Q, z * Q + other % Q)

    zb[s_rows, n_cols] = zm[0]

    holds_w = z // HW == n

    @pl.when(holds_w)
    def _():
        for child in range(2):
            @pl.when(z != planes[1 + child])
            def _():
                arrived(wm.at[child], "WM", child)

            @pl.loop(1, C)
            def _(k):
                other = (flat + k) % C
                share = flip(other // Q, other % Q)
                push(
                    wm.at[child, :, pl.ds(pl.multiple_of(share * NQ, NQ), NQ)],
                    wb.at[child, s_rows], "WB", other // Q, z * Q + other % Q, child,
                )

            wb[child, s_rows] = wm[child, :, n_cols]

    rows_sum(3, 1, 1)
    rows_sum(4, 2, 2)
    arrived(db.at[: (Q - 1) * GC], "D")
    arrived(fb.at[0, : (C - 1) * SP], "ZB")
    zb[...] = db[...] - zb[...]
    out_ref[3] = zb[n_rows]
    for child in range(2):
        @pl.when(holds_w)
        def _():
            arrived(wb.at[child, : (R - 1) * SP], "WB", child)

        @pl.when(jnp.logical_not(holds_w))
        def _():
            arrived(wb.at[child], "WB", child)

        eb[child] = wb[child] + mm(zb[...], gc[child])
        ge[child] = mm_t(gn[child], eb[child]).reshape(R, R, SP, NQ)
        for k in range(1, R):
            dest = (z + k) % R
            push(ge.at[child, dest, r], gz.at[child, R - 1 - k], "GZ", r, dest * Q + q, child)
        for k in range(1, Q):
            other = (q + k) % Q
            push(
                eb.at[child, pl.ds(pl.multiple_of(other * GC, GC), GC)], uo.at[child, :, n_cols],
                "UO", r, z * Q + other,
            )
        uo[child, :, n_cols] = eb[child, n_rows]

    spread(3, 1)
    spread(4, 2)

    o_rows = pl.ds(pl.multiple_of(r % (R // Q) * SP, SP), SP)
    o_place = r // (R // Q)
    for child in range(2):
        @pl.when(z != planes[3 + child])
        def _():
            arrived(zm.at[1 + child], "ZM", 1 + child)

        arrived(gz.at[child], "GZ", child)
        total = ge[child, z, r] - zm[1 + child]
        for k in range(R - 1):
            total = total + gz[child, k]
        zp[child] = total
        for k in range(1, R):
            push(
                zp.at[child], zo.at[child, o_rows, n_cols], "ZO", (r + k) % R, z * Q + o_place, child
            )

        @pl.when(q == o_place)
        def _():
            zo[child, o_rows, n_cols] = zp[child]

        @pl.when(q != o_place)
        def _():
            push(zp.at[child], zo.at[child, o_rows, n_cols], "ZO", r, z * Q + o_place, child)

    arrived(yo.at[:, :, : (Q - 1) * NQ], "YO")
    out_ref[1:3] = yo[...]
    arrived(uo.at[:, :, : (Q - 1) * NQ], "UO")
    out_ref[6:8] = -uo[...]
    for child in range(2):
        @pl.when(q == o_place)
        def _():
            arrived(rb.at[child, 0, : (R - 1) * SP], "ZO", child)

        @pl.when(q != o_place)
        def _():
            arrived(rb.at[child, 0, : R * SP], "ZO", child)

        out_ref[4 + child] = d_ref[1 + child] + zo[child]

    sent(a_ref, "A", 0)
    sent(a_ref, "A", 1)
    sent(a_ref, "A", 2)
    for k in range(HR):
        sent(gc.at[:, my_rows], "GP", k)
    for k in range(R - 1 - HR):
        sent(gc.at[:, my_rows], "GM", k)
    sent(gn.at[:, : (Q - 1) * GC], "GN")
    sent(db.at[: (Q - 1) * GC], "D")
    sent(y0n.at[:, : (Q - 1) * NQ], "Y0")
    sent(yo.at[:, :, : (Q - 1) * NQ], "YO")
    sent(uo.at[:, :, : (Q - 1) * NQ], "UO")
    sent(fb.at[0, : (C - 1) * SP], "ZB")
    for j in range(3):
        @pl.when(near)
        def _():
            sent(fb.at[j, : 4 * HZ], "FS", j)

        @pl.when(above | below)
        def _():
            sent(fb.at[j, : 2 * HZ], "FS", j)

        @pl.when(r != z)
        def _():
            sent(fb.at[j, : (R - 2) * HZ], "FA", j)

        sent(xb.at[j], "X", j)
        sent(rb.at[j], "RB", j)

    @pl.when(r == partner)
    def _():
        sent(fb.at[:, : (R - 2) * HZ], "FX")

    for j in range(3):
        targets = planes[:3] if j == 0 else planes[2 + j : 3 + j]
        inside = functools.reduce(jnp.logical_or, [z == plane for plane in targets])

        @pl.when(inside)
        def _():
            if len(targets) > 1:
                sent(yu.at[: (len(targets) - 1) * HZ], "YU", j)

        @pl.when(jnp.logical_not(inside))
        def _():
            sent(yu.at[: len(targets) * HZ], "YU", j)

    for unit in range(5):
        @pl.when(z == planes[unit])
        def _():
            if unit in (1, 2):
                sent(trw, "TR")

                @pl.when(z // HW == n)
                def _():
                    if HW > 1:
                        sent(tsw.at[: HW - 1], "WM", unit - 1)

                @pl.when(z // HW != n)
                def _():
                    sent(tsw, "WM", unit - 1)
            else:
                place = (0, None, None, 1, 2)[unit]
                sent(tr, "TR")
                sent(ts.at[: R - 1], "ZM", place)

    for child in range(2):
        @pl.when(holds_w)
        def _():
            sent(fb.at[0, : (C - 1) * SP], "WB", child)

        sent(gz.at[child], "GZ", child)

        @pl.when(q == o_place)
        def _():
            sent(rb.at[child, 0, : (R - 1) * SP], "ZO", child)

        @pl.when(q != o_place)
        def _():
            sent(rb.at[child, 0, : R * SP], "ZO", child)


def shards(region_inverse, factor_cols, parent_factor, diag_inverse, listed):
    R = lax.axis_size("row")
    C = lax.axis_size("col")
    W = factor_cols.shape[2]
    Q = C // R
    NQ, HZ, GC = W // Q, W // R, W // C
    SP = HZ // R
    HW = NQ // HZ
    planes = (0, 2, 5, 3, 7)
    f32 = jnp.float32
    vmem = pl.BlockSpec(memory_space=pltpu.VMEM)
    smem = pl.BlockSpec(memory_space=pltpu.SMEM)
    scratch = [
        (W, W), (3, W, NQ), (3, W, W), (3, W, NQ), (3, 3, HZ, NQ), (3, 2, HZ, NQ), (3, 4, HZ, NQ),
        (2, W, NQ), (2, HZ, W), (HZ, W), (HZ, W), (3, HZ, NQ), (2, HZ, NQ), (2, GC, W), (W, NQ),
        (R, R, SP, NQ), (HW, R, SP, W), (R - 1, R, SP, NQ), (R - 1, HW, SP, W),
        (R, SP, NQ), (HW, SP, W),
        (3, SP, NQ), (HZ, W), (2, SP, W), (2, HZ, NQ), (2, HZ, NQ), (2, GC, W),
        (2, R, R, SP, NQ), (2, R - 1, SP, NQ), (2, SP, NQ), (2, GC, W),
    ]
    whole = pl.pallas_call(
        functools.partial(kernel, R, C, W, planes),
        out_shape=jax.ShapeDtypeStruct((8, GC, W), f32),
        in_specs=[vmem, pl.BlockSpec(memory_space=pl.ANY), vmem, vmem, smem],
        out_specs=vmem,
        scratch_shapes=[pltpu.VMEM(shape, f32) for shape in scratch]
        + [pltpu.SemaphoreType.DMA((N_SEM,)), pltpu.SemaphoreType.DMA((N_SEM,))],
        compiler_params=pltpu.CompilerParams(
            collective_id=0, has_side_effects=True, vmem_limit_bytes=24 * 2**20
        ),
    )(region_inverse, factor_cols, parent_factor, diag_inverse, listed)
    return pl.pallas_call(
        split,
        out_shape=(
            jax.ShapeDtypeStruct((3, GC, W), f32),
            jax.ShapeDtypeStruct((3, GC, W), f32),
            jax.ShapeDtypeStruct((2, GC, W), f32),
        ),
        in_specs=[vmem],
        out_specs=(vmem, vmem, vmem),
        compiler_params=pltpu.CompilerParams(vmem_limit_bytes=4 * 2**20),
    )(whole)


def split(whole_ref, col_ref, diag_ref, par_ref):
    col_ref[...] = whole_ref[0:3]
    diag_ref[...] = whole_ref[3:6]
    par_ref[...] = whole_ref[6:8]


def solution(mesh):
    in_specs = (
        P("row", "col"),
        P(None, "row", None),
        P(None, "col", None),
        P(None, "col", None),
        P(),
    )
    out_specs = (P(None, ("row", "col"), None), P(None, "col", None), P(None, "col", None))
    return jax.shard_map(shards, mesh=mesh, in_specs=in_specs, out_specs=out_specs, check_vma=False)
```

```python
import functools

import jax
import jax.numpy as jnp
from jax import lax
from jax.experimental import pallas as pl
from jax.experimental.pallas import tpu as pltpu
from jax.sharding import PartitionSpec as P

MESH = pl.DeviceIdType.MESH
HIGH = lax.Precision.HIGHEST

SIZES = dict(
    A=3, FS=3, FA=3, FX=1, GN=1, G0=1, D=1, GP=4, GM=3, X=3, RB=3, Y0=1, YO=1, YU=3, ZM=3, ZB=1, WM=2,
    WB=2, UO=1, GZ=2, ZO=2, FB=3, FV=1, LA=1, LG=1, LC=1, LD=1,
)
BASE = {}
N_SEM = 0
for _name, _size in SIZES.items():
    BASE[_name] = N_SEM
    N_SEM += _size

OFFSET = {1: 0, 3: 0, 4: 0, 2: -1, 7: -1, 5: 1, 6: 1}


def halves(x):
    hi = x.astype(jnp.bfloat16)
    return hi, (x - hi.astype(jnp.float32)).astype(jnp.bfloat16)


def dot(a, b, dims=((1,), (0,))):
    return lax.dot_general(a, b, (dims, ((), ())), preferred_element_type=jnp.float32)


def mm3(a_hi, a_lo, b):
    b_hi, b_lo = halves(b)
    cols = b.shape[1]
    both = dot(a_hi, jnp.concatenate([b_hi, b_lo], axis=1))
    return both[:, :cols] + (both[:, cols:] + dot(a_lo, b_hi))


def mm(a, b):
    return mm3(*halves(a), b)


def mm_t(a, b):
    return lax.dot_general(
        a, b, (((0,), (0,)), ((), ())), precision=HIGH, preferred_element_type=jnp.float32
    )


def kernel(
    R, C, W, planes,
    a_ref, f_ref, g_ref, d_ref, listed_ref,
    out_ref,
    abuf, fb, fv, pb, xb, rl, rb, gc, gn, db, dv, y0n, yc, xc, yo, yu, tp, tpw, zr, wr,
    zm, zb, wm, wb, eb, uo, ge, gz, zp, zo, ah, al, fh, fl, send, recv,
):
    Q = C // R
    NQ, HZ, GC = W // Q, W // R, W // C
    SP = HZ // R
    HW = NQ // HZ
    HR = R // 2
    r = lax.axis_index("row")
    c = lax.axis_index("col")
    z = c // Q
    q = c % Q

    def flip(row, place):
        return 2 * ((place // 2 + row // HR) % 2) + place % 2

    def at(row, k):
        return (row // HR + k // HR) % 2 * HR + (row % HR + k % HR) % HR

    n = flip(r, q)
    partner = at(z, HR)
    core = q % 2
    sibling = q + 1 - 2 * core
    across = (q + 2) % Q
    n_cols = pl.ds(pl.multiple_of(n * NQ, NQ), NQ)

    def piece(i):
        return pl.ds(pl.multiple_of(i * HZ, HZ), HZ)

    my_rows = piece(z)

    def push(src, dst, s, row, col, k=0):
        s = BASE[s] + k
        pltpu.make_async_remote_copy(
            src_ref=src, dst_ref=dst, send_sem=send.at[s], recv_sem=recv.at[s],
            device_id=(row, col), device_id_type=MESH,
        ).start()

    def arrived(view, s, k=0):
        pltpu.make_async_copy(view, view, recv.at[BASE[s] + k]).wait()

    def sent(view, s, k=0):
        pltpu.make_async_copy(view, view, send.at[BASE[s] + k]).wait()

    def weight(member, block):
        return listed_ref[member, block].astype(jnp.float32)

    barrier = pltpu.get_barrier_semaphore()

    def greet(row, col):
        pl.semaphore_signal(barrier, inc=1, device_id=(row, col), device_id_type=MESH)

    for k in range(1, R):
        i = at(r, k)
        greet(i, z * Q + flip(i, n))
    for k in range(1, R):
        greet(r, (z + k) % R * Q + q)
    for k in range(1, Q):
        greet(r, z * Q + (q + k) % Q)
    for k, offset in OFFSET.items():
        if offset:
            @pl.when(at(z, k) == r)
            def _():
                greet(z, (z + offset) % R * Q + flip(z, n))

    near = z == r
    above = z == (r + 1) % R
    below = (z + 1) % R == r
    a_cols = pl.ds(pl.multiple_of(q * NQ, NQ), NQ)
    x_cols = pl.ds(pl.multiple_of(across * NQ, NQ), NQ)
    n_rows = pl.ds(pl.multiple_of(q * GC, GC), GC)
    g_rows = pl.ds(pl.multiple_of(c * GC, GC), GC)

    def local(src, dst, s, k=0):
        pltpu.make_async_copy(src, dst, recv.at[BASE[s] + k]).start()

    def loaded(view, s, k=0):
        pltpu.make_async_copy(view, view, recv.at[BASE[s] + k]).wait()

    for unit, member in enumerate((0, 1, 2, 1, 2)):
        @pl.when(z == planes[unit])
        def _():
            local(f_ref.at[member], fv, "FV")

    local(g_ref.at[:, :, n_cols], gc.at[:, g_rows], "LC")
    local(a_ref, abuf.at[:, a_cols], "LA")

    @pl.when(near)
    def _():
        for j in range(3):
            local(f_ref.at[j, :, n_cols], fb.at[j], "FB", j)

    local(g_ref, gn.at[:, n_rows], "LG")
    local(d_ref, dv, "LD")
    in_cols = functools.reduce(jnp.logical_or, [z == planes[unit] for unit in (0, 3, 4)])
    in_rows = functools.reduce(jnp.logical_or, [z == planes[unit] for unit in (1, 2)])

    @pl.when(in_cols)
    def _():
        loaded(fv, "FV")
        fh[...], fl[...] = halves(fv[...].T)

    @pl.when(in_rows)
    def _():
        loaded(fv, "FV")
        fh[...], fl[...] = halves(fv[...])

    peers = 2 * (R - 1) + Q - 1

    @pl.when(above | below)
    def _():
        pl.semaphore_wait(barrier, peers + 2)

    @pl.when(jnp.logical_not(above | below))
    def _():
        pl.semaphore_wait(barrier, peers)

    for offset, here in ((0, near), (1, above), (-1, below)):
        @pl.when(here)
        def _():
            for j in range(3):
                for k, source in OFFSET.items():
                    if source == offset:
                        i = at(r, k)
                        push(
                            f_ref.at[j, piece(i), n_cols], fb.at[j, piece(i)], "FS",
                            i, r * Q + flip(i, n), j,
                        )
                if offset == 0:
                    push(
                        f_ref.at[j, piece(z), n_cols], fb.at[j, piece(z)], "FS",
                        partner, z * Q + flip(partner, n), j,
                    )

    for k in range(1, Q):
        other = (q + k) % Q
        share = flip(r, other)
        push(
            g_ref.at[:, :, pl.ds(pl.multiple_of(share * NQ, NQ), NQ)], gc.at[:, g_rows], "G0",
            r, z * Q + other,
        )
    push(a_ref, abuf.at[:, a_cols], "A", r, z * Q + across, 1)
    push(a_ref, abuf.at[:, a_cols], "A", r, z * Q + sibling, 0)

    def forward(j):
        @pl.when(r != z)
        def _():
            @pl.when(r == partner)
            def _():
                arrived(fb.at[j, : 2 * HZ], "FS", j)

            @pl.when(r != partner)
            def _():
                arrived(fb.at[j, :HZ], "FS", j)

            for k in range(1, R):
                i = at(r, k)

                @pl.when(i != z)
                def _():
                    push(fb.at[j, piece(r)], fb.at[j, piece(r)], "FA", i, z * Q + flip(i, n), j)

                    @pl.when(r == partner)
                    def _():
                        pltpu.make_async_remote_copy(
                            src_ref=fb.at[j, piece(z)], dst_ref=fb.at[j, piece(z)],
                            send_sem=send.at[BASE["FX"]], recv_sem=recv.at[BASE["FA"] + j],
                            device_id=(i, z * Q + flip(i, n)), device_id_type=MESH,
                        ).start()

    def g_step(k):
        if k == 0:
            loaded(gc.at[:, g_rows], "LC")
            arrived(gc.at[:, : (Q - 1) * GC], "G0")
        up = gc.at[:, piece((z - k) % R)]
        down = gc.at[:, piece((z + k) % R)]
        if k:
            arrived(up, "GP", k - 1)
        push(up, up, "GP", r, (z + 1) % R * Q + q, k)
        if k < R - 1 - HR:
            if k:
                arrived(down, "GM", k - 1)
            push(down, down, "GM", r, (z - 1) % R * Q + q, k)

    s = 1 - 2 * core

    def along(k):
        return (z + s * k) % R

    def product(j):
        @pl.when(r == z)
        def _():
            loaded(fb.at[j], "FB", j)

        @pl.when((r != z) & (r != partner))
        def _():
            arrived(fb.at[j, : (R - 1) * HZ], "FA", j)

        @pl.when(r == partner)
        def _():
            arrived(fb.at[j, : (R - 2) * HZ], "FA", j)

        pb[j] = mm3(ah[...], al[...], fb[j]) * weight(j, z)

        def part(k):
            return pb.at[j, piece(along(k))]

        push(part(4), xb.at[j, 0], "X", r, along(2) * Q + q, j)
        push(part(3), xb.at[j, 1], "X", r, along(1) * Q + q, j)
        push(part(-3), xb.at[j, 2], "X", r, along(-1) * Q + q, j)
        push(part(1), rb.at[j, 0], "RB", r, along(1) * Q + q, j)
        push(part(-1), rb.at[j, 1], "RB", r, along(-1) * Q + q, j)

    def relay(j):
        arrived(xb.at[j], "X", j)
        rl[j, 0] = pb[j, piece(along(2))] + xb[j, 0] + xb[j, 1]
        rl[j, 1] = pb[j, piece(along(-2))] + xb[j, 2]
        push(rl.at[j, 0], rb.at[j, 2], "RB", r, along(2) * Q + q, j)
        push(rl.at[j, 1], rb.at[j, 3], "RB", r, along(-2) * Q + q, j)

    g_step(0)
    forward(0)
    g_step(1)
    forward(1)
    g_step(2)
    forward(2)
    arrived(abuf.at[:, x_cols], "A", 1)
    push(abuf.at[:, x_cols], abuf.at[:, x_cols], "A", r, z * Q + sibling, 2)
    loaded(abuf.at[:, a_cols], "LA")
    for k in range(1, Q):
        push(g_ref, gn.at[:, n_rows], "GN", r, z * Q + (q + k) % Q)
        push(d_ref.at[0], db.at[n_rows], "D", r, z * Q + (q + k) % Q)
    g_step(3)
    arrived(abuf.at[:, a_cols], "A", 0)
    arrived(abuf.at[:, a_cols], "A", 2)
    ah[...], al[...] = halves(abuf[...])
    product(0)
    product(1)
    relay(0)
    product(2)
    relay(1)

    def summed(j):
        arrived(rb.at[j], "RB", j)
        return ((pb[j, my_rows] + rb[j, 0]) + (rb[j, 1] + rb[j, 2])) + rb[j, 3]

    def to_unit(j, plane):
        @pl.when(z != plane)
        def _():
            push(yc.at[j], yu.at[my_rows], "YU", r, plane * Q + q, j)

        @pl.when(z == plane)
        def _():
            yu[my_rows] = yc[j]

    yc[0] = -weight(0, r) * summed(0)
    for k in range(1, Q):
        push(yc.at[0], y0n.at[:, n_cols], "Y0", r, z * Q + (q + k) % Q)
    for plane in planes[:3]:
        to_unit(0, plane)
    y0n[:, n_cols] = yc[0]
    relay(2)
    arrived(y0n.at[:, : (Q - 1) * NQ], "Y0")
    out_ref[0] = y0n[n_rows]
    arrived(gc.at[:, piece((z - HR) % R)], "GP", HR - 1)
    arrived(gc.at[:, piece((z + HR - 1) % R)], "GM", HR - 2)
    for j in (1, 2):
        xc[j - 1] = mm(y0n[...], gc[j - 1])

    def child_columns(j):
        yc[j] = -weight(j, r) * (summed(j) + xc[j - 1])
        to_unit(j, planes[2 + j])
        for k in range(1, Q):
            other = (q + k) % Q
            push(
                yc.at[j, pl.ds(pl.multiple_of(other * GC, GC), GC)], yo.at[j - 1, :, n_cols],
                "YO", r, z * Q + other,
            )
        yo[j - 1, :, n_cols] = yc[j, n_rows]

    def rows_sum(unit, source, place):
        @pl.when(z == planes[unit])
        def _():
            arrived(yu.at[: (R - 1) * HZ], "YU", source)
            tp[...] = mm3(fh[...], fl[...], yu[...]).reshape(R, R, SP, NQ)
            zr[place, 0] = tp[z, r]

            @pl.loop(1, R * R)
            def _(t):
                i = at(r, t // R)
                dest = (z + t % R) % R
                push(tp.at[dest, i], zr.at[place, t // R], "ZM", i, dest * Q + flip(i, n), place)

    def cross_sum(unit, child):
        @pl.when(z == planes[unit])
        def _():
            arrived(yu.at[: (R - 1) * HZ], "YU", 0)
            y_hi, y_lo = halves(yu[...].T)
            total = dot(y_hi, fh[...]) + (dot(y_hi, fl[...]) + dot(y_lo, fh[...]))
            tpw[...] = (total * weight(1 + child, r)).reshape(HW, R, SP, W)

            @pl.loop(0, R * HW)
            def _(t):
                i = at(r, t // HW)
                dest = n * HW + t % HW
                own = (t < HW) & (dest == z)

                @pl.when(own)
                def _():
                    wr[child, 0] = tpw[t % HW, r]

                @pl.when(jnp.logical_not(own))
                def _():
                    push(
                        tpw.at[t % HW, i], wr.at[child, t // HW], "WM", i, dest * Q + flip(i, n), child
                    )

    def added(place, plane):
        @pl.when(z == plane)
        def _():
            arrived(zr.at[place, : R - 1], "ZM", place)

        @pl.when(z != plane)
        def _():
            arrived(zr.at[place], "ZM", place)

        return functools.reduce(jnp.add, [zr[place, k] for k in range(R)])

    rows_sum(0, 0, 0)
    cross_sum(1, 0)
    cross_sum(2, 1)
    child_columns(1)
    child_columns(2)
    rows_sum(3, 1, 1)
    rows_sum(4, 2, 2)

    s_rows = pl.ds(pl.multiple_of(r * SP, SP), SP)
    flat = r * Q + q

    zm[...] = added(0, planes[0])

    @pl.loop(1, C)
    def _(k):
        other = (flat + k) % C
        push(zm, zb.at[s_rows, n_cols], "ZB", other // Q, z * Q + other % Q)

    zb[s_rows, n_cols] = zm[...]

    holds_w = z // HW == n

    @pl.when(holds_w)
    def _():
        for child in range(2):
            @pl.when(z == planes[1 + child])
            def _():
                arrived(wr.at[child, : R - 1], "WM", child)

            @pl.when(z != planes[1 + child])
            def _():
                arrived(wr.at[child], "WM", child)

            wm[child] = functools.reduce(jnp.add, [wr[child, k] for k in range(R)])

            @pl.loop(1, C)
            def _(k):
                other = (flat + k) % C
                share = flip(other // Q, other % Q)
                push(
                    wm.at[child, :, pl.ds(pl.multiple_of(share * NQ, NQ), NQ)],
                    wb.at[child, s_rows], "WB", other // Q, z * Q + other % Q, child,
                )

            wb[child, s_rows] = wm[child, :, n_cols]

    loaded(dv, "LD")
    loaded(gn.at[:, n_rows], "LG")
    arrived(gn.at[:, : (Q - 1) * GC], "GN")
    arrived(db.at[: (Q - 1) * GC], "D")
    db[n_rows] = dv[0]
    arrived(fb.at[0, : (C - 1) * SP], "ZB")
    zb[...] = db[...] - zb[...]
    out_ref[3] = zb[n_rows]
    for child in range(2):
        @pl.when(holds_w)
        def _():
            arrived(wb.at[child, : (R - 1) * SP], "WB", child)

        @pl.when(jnp.logical_not(holds_w))
        def _():
            arrived(wb.at[child], "WB", child)

        eb[child] = wb[child] + mm(zb[...], gc[child])
        ge[child] = mm_t(gn[child], eb[child]).reshape(R, R, SP, NQ)
        for k in range(1, R):
            dest = (z + k) % R
            push(ge.at[child, dest, r], gz.at[child, R - 1 - k], "GZ", r, dest * Q + q, child)
        for k in range(1, Q):
            other = (q + k) % Q
            push(
                eb.at[child, pl.ds(pl.multiple_of(other * GC, GC), GC)], uo.at[child, :, n_cols],
                "UO", r, z * Q + other,
            )
        uo[child, :, n_cols] = eb[child, n_rows]

    o_rows = pl.ds(pl.multiple_of(r % (R // Q) * SP, SP), SP)
    o_place = r // (R // Q)
    for child in range(2):
        share = added(1 + child, planes[3 + child])
        arrived(gz.at[child], "GZ", child)
        total = ge[child, z, r] - share
        for k in range(R - 1):
            total = total + gz[child, k]
        zp[child] = total
        for k in range(1, R):
            push(
                zp.at[child], zo.at[child, o_rows, n_cols], "ZO", (r + k) % R, z * Q + o_place, child
            )

        @pl.when(q == o_place)
        def _():
            zo[child, o_rows, n_cols] = zp[child]

        @pl.when(q != o_place)
        def _():
            push(zp.at[child], zo.at[child, o_rows, n_cols], "ZO", r, z * Q + o_place, child)

    arrived(yo.at[:, :, : (Q - 1) * NQ], "YO")
    out_ref[1:3] = yo[...]
    arrived(uo.at[:, :, : (Q - 1) * NQ], "UO")
    out_ref[6:8] = -uo[...]
    for child in range(2):
        @pl.when(q == o_place)
        def _():
            arrived(rb.at[child, 0, : (R - 1) * SP], "ZO", child)

        @pl.when(q != o_place)
        def _():
            arrived(rb.at[child, 0, : R * SP], "ZO", child)

        out_ref[4 + child] = dv[1 + child] + zo[child]

    for k in range(3):
        sent(abuf.at[:, a_cols], "A", k)
    sent(gc.at[:, : (Q - 1) * GC], "G0")
    for k in range(HR):
        sent(gc.at[:, my_rows], "GP", k)
    for k in range(R - 1 - HR):
        sent(gc.at[:, my_rows], "GM", k)
    sent(gn.at[:, : (Q - 1) * GC], "GN")
    sent(db.at[: (Q - 1) * GC], "D")
    sent(y0n.at[:, : (Q - 1) * NQ], "Y0")
    sent(yo.at[:, :, : (Q - 1) * NQ], "YO")
    sent(uo.at[:, :, : (Q - 1) * NQ], "UO")
    sent(fb.at[0, : (C - 1) * SP], "ZB")
    for j in range(3):
        @pl.when(near)
        def _():
            sent(fb.at[j, : 4 * HZ], "FS", j)

        @pl.when(above | below)
        def _():
            sent(fb.at[j, : 2 * HZ], "FS", j)

        @pl.when(r != z)
        def _():
            sent(fb.at[j, : (R - 2) * HZ], "FA", j)

        sent(xb.at[j], "X", j)
        sent(rb.at[j], "RB", j)

    @pl.when(r == partner)
    def _():
        sent(fb.at[:, : (R - 2) * HZ], "FX")

    for j in range(3):
        targets = planes[:3] if j == 0 else planes[2 + j : 3 + j]
        inside = functools.reduce(jnp.logical_or, [z == plane for plane in targets])

        @pl.when(inside)
        def _():
            if len(targets) > 1:
                sent(yu.at[: (len(targets) - 1) * HZ], "YU", j)

        @pl.when(jnp.logical_not(inside))
        def _():
            sent(yu.at[: len(targets) * HZ], "YU", j)

    for unit, place in ((0, 0), (3, 1), (4, 2)):
        @pl.when(z == planes[unit])
        def _():
            sent(fb.at[0, : (R * R - 1) * SP], "ZM", place)

    for child in range(2):
        @pl.when((z == planes[1 + child]) & holds_w)
        def _():
            sent(fv.at[: (R * HW - 1) * SP], "WM", child)

        @pl.when((z == planes[1 + child]) & jnp.logical_not(holds_w))
        def _():
            sent(fv.at[: R * HW * SP], "WM", child)

    for child in range(2):
        @pl.when(holds_w)
        def _():
            sent(fb.at[0, : (C - 1) * SP], "WB", child)

        sent(gz.at[child], "GZ", child)

        @pl.when(q == o_place)
        def _():
            sent(rb.at[child, 0, : (R - 1) * SP], "ZO", child)

        @pl.when(q != o_place)
        def _():
            sent(rb.at[child, 0, : R * SP], "ZO", child)


def shards(region_inverse, factor_cols, parent_factor, diag_inverse, listed):
    R = lax.axis_size("row")
    C = lax.axis_size("col")
    W = factor_cols.shape[2]
    Q = C // R
    NQ, HZ, GC = W // Q, W // R, W // C
    SP = HZ // R
    HW = NQ // HZ
    planes = (0, 2, 5, 3, 7)
    f32 = jnp.float32
    vmem = pl.BlockSpec(memory_space=pltpu.VMEM)
    smem = pl.BlockSpec(memory_space=pltpu.SMEM)
    scratch = [
        (W, W), (3, W, NQ), (W, W), (3, W, NQ), (3, 3, HZ, NQ), (3, 2, HZ, NQ), (3, 4, HZ, NQ),
        (2, W, NQ), (2, HZ, W), (HZ, W), (3, GC, W), (HZ, W), (3, HZ, NQ), (2, HZ, NQ), (2, GC, W),
        (W, NQ), (R, R, SP, NQ), (HW, R, SP, W), (3, R, SP, NQ), (2, R, SP, W),
        (SP, NQ), (HZ, W), (2, SP, W), (2, HZ, NQ), (2, HZ, NQ), (2, GC, W),
        (2, R, R, SP, NQ), (2, R - 1, SP, NQ), (2, SP, NQ), (2, GC, W),
    ]
    hbm = pl.BlockSpec(memory_space=pl.ANY)
    whole = pl.pallas_call(
        functools.partial(kernel, R, C, W, planes),
        out_shape=jax.ShapeDtypeStruct((8, GC, W), f32),
        in_specs=[hbm, hbm, hbm, hbm, smem],
        out_specs=vmem,
        scratch_shapes=[pltpu.VMEM(shape, f32) for shape in scratch]
        + [pltpu.VMEM((W, W), jnp.bfloat16)] * 4
        + [pltpu.SemaphoreType.DMA((N_SEM,)), pltpu.SemaphoreType.DMA((N_SEM,))],
        compiler_params=pltpu.CompilerParams(
            collective_id=0, has_side_effects=True, vmem_limit_bytes=60 * 2**20
        ),
    )(region_inverse, factor_cols, parent_factor, diag_inverse, listed)
    return pl.pallas_call(
        split,
        out_shape=(
            jax.ShapeDtypeStruct((3, GC, W), f32),
            jax.ShapeDtypeStruct((3, GC, W), f32),
            jax.ShapeDtypeStruct((2, GC, W), f32),
        ),
        in_specs=[vmem],
        out_specs=(vmem, vmem, vmem),
        compiler_params=pltpu.CompilerParams(vmem_limit_bytes=4 * 2**20),
    )(whole)


def split(whole_ref, col_ref, diag_ref, par_ref):
    col_ref[...] = whole_ref[0:3]
    diag_ref[...] = whole_ref[3:6]
    par_ref[...] = whole_ref[6:8]


def solution(mesh):
    in_specs = (
        P("row", "col"),
        P(None, "row", None),
        P(None, "col", None),
        P(None, "col", None),
        P(),
    )
    out_specs = (P(None, ("row", "col"), None), P(None, "col", None), P(None, "col", None))
    return jax.shard_map(shards, mesh=mesh, in_specs=in_specs, out_specs=out_specs, check_vma=False)
```

```python
import functools

import jax
import jax.numpy as jnp
from jax import lax
from jax.experimental import pallas as pl
from jax.experimental.pallas import tpu as pltpu
from jax.sharding import PartitionSpec as P

MESH = pl.DeviceIdType.MESH
HIGH = lax.Precision.HIGHEST

SIZES = dict(
    A=3, FS=3, FA=3, FX=1, GN=1, G0=1, D=1, GP=4, GM=3, X=3, RB=3, Y0=1, YO=1, YU=3, ZM=3, ZB=1, WM=2,
    WB=2, UO=1, GZ=2, ZO=2, FB=3, FV=1, LA=1, LG=1, LC=1, LD=1,
)
BASE = {}
N_SEM = 0
for _name, _size in SIZES.items():
    BASE[_name] = N_SEM
    N_SEM += _size

OFFSET = {1: 0, 3: 0, 4: 0, 2: -1, 7: -1, 5: 1, 6: 1}


def halves(x):
    hi = x.astype(jnp.bfloat16)
    return hi, (x - hi.astype(jnp.float32)).astype(jnp.bfloat16)


def dot(a, b, dims=((1,), (0,))):
    return lax.dot_general(a, b, (dims, ((), ())), preferred_element_type=jnp.float32)


def mm3(a_hi, a_lo, b):
    b_hi, b_lo = halves(b)
    cols = b.shape[1]
    both = dot(a_hi, jnp.concatenate([b_hi, b_lo], axis=1))
    return both[:, :cols] + (both[:, cols:] + dot(a_lo, b_hi))


def mm(a, b):
    return mm3(*halves(a), b)


def mm_t(a, b):
    return lax.dot_general(
        a, b, (((0,), (0,)), ((), ())), precision=HIGH, preferred_element_type=jnp.float32
    )


def kernel(
    R, C, W, planes,
    a_ref, f_ref, g_ref, d_ref, listed_ref,
    out_ref,
    abuf, fb, fv, pb, xb, rl, rb, gc, gn, db, dv, y0n, yc, xc, yo, yu, tp, tpw, zr, wr,
    zm, zb, wm, wb, eb, uo, ge, gz, zp, zo, ah, al, fh, fl, send, recv,
):
    Q = C // R
    NQ, HZ, GC = W // Q, W // R, W // C
    SP = HZ // R
    HW = NQ // HZ
    HR = R // 2
    r = lax.axis_index("row")
    c = lax.axis_index("col")

    def wrap(value, size):
        return jnp.where(value >= size, value - size, value)

    z = lax.div(c, Q)
    q = c - z * Q
    half = lax.div(r, HR)
    y = r - half * HR
    pair = lax.div(q, 2)
    core = q - pair * 2
    z_half = lax.div(z, HR)
    z_y = z - z_half * HR
    kind = jnp.where(pair == half, 0, 1)
    across = 2 * (1 - pair) + core
    sibling = 2 * pair + 1 - core
    diagonal = 2 * (1 - pair) + 1 - core
    node = (q, sibling, across, diagonal)
    n = 2 * kind + core
    shares = (n, 2 * kind + 1 - core, 2 * (1 - kind) + core, 2 * (1 - kind) + 1 - core)
    other_shares = (shares[2], shares[3], shares[0], shares[1])
    ys = [wrap(y + k, HR) if k else y for k in range(HR)]
    rows = [half * HR + v for v in ys] + [(1 - half) * HR + v for v in ys]
    qs = [q] * HR + [across] * HR
    zs = [wrap(z + k, R) if k else z for k in range(R)]
    zc = [v * Q for v in zs]
    base = zc[0]
    zd = [zs[k] if k % HR == 0 else jnp.where(core == 0, zs[k], zs[R - k]) for k in range(R)]
    far = half != z_half
    place_of = wrap(y - z_y + HR, HR) + jnp.where(far, HR, 0)
    partner = z + HR - 2 * HR * z_half

    def span(i, size):
        return pl.ds(pl.multiple_of(i * size, size), size)

    def piece(i):
        return span(i, HZ)

    n_cols = span(n, NQ)
    my_rows = piece(z)

    def push(src, dst, s, row, col, k=0):
        s = BASE[s] + k
        pltpu.make_async_remote_copy(
            src_ref=src, dst_ref=dst, send_sem=send.at[s], recv_sem=recv.at[s],
            device_id=(row, col), device_id_type=MESH,
        ).start()

    def arrived(view, s, k=0):
        pltpu.make_async_copy(view, view, recv.at[BASE[s] + k]).wait()

    def sent(view, s, k=0):
        pltpu.make_async_copy(view, view, send.at[BASE[s] + k]).wait()

    def weight(member, block):
        return listed_ref[member, block].astype(jnp.float32)

    barrier = pltpu.get_barrier_semaphore()

    def greet(row, col):
        pl.semaphore_signal(barrier, inc=1, device_id=(row, col), device_id_type=MESH)

    for k in range(1, R):
        greet(rows[k], base + qs[k])
    for k in range(1, R):
        greet(r, zc[k] + q)
    for k in range(1, Q):
        greet(r, base + node[k])
    q_source = jnp.where(far, across, q)
    for step in (1, -1):
        ours = functools.reduce(
            jnp.logical_or, [place_of == k for k, offset in OFFSET.items() if offset == step]
        )

        @pl.when(ours)
        def _():
            greet(z, zc[step % R] + q_source)

    near = z == r
    above = zs[R - 1] == r
    below = zs[1] == r
    a_cols = span(q, NQ)
    x_cols = span(across, NQ)
    n_rows = span(q, GC)
    g_rows = span(c, GC)

    def local(src, dst, s, k=0):
        pltpu.make_async_copy(src, dst, recv.at[BASE[s] + k]).start()

    def loaded(view, s, k=0):
        pltpu.make_async_copy(view, view, recv.at[BASE[s] + k]).wait()

    for unit, member in enumerate((0, 1, 2, 1, 2)):
        @pl.when(z == planes[unit])
        def _():
            local(f_ref.at[member], fv, "FV")

    local(g_ref.at[:, :, n_cols], gc.at[:, g_rows], "LC")
    local(a_ref, abuf.at[:, a_cols], "LA")

    @pl.when(near)
    def _():
        for j in range(3):
            local(f_ref.at[j, :, n_cols], fb.at[j], "FB", j)

    local(g_ref, gn.at[:, n_rows], "LG")
    local(d_ref, dv, "LD")
    in_cols = functools.reduce(jnp.logical_or, [z == planes[unit] for unit in (0, 3, 4)])
    in_rows = functools.reduce(jnp.logical_or, [z == planes[unit] for unit in (1, 2)])

    @pl.when(in_cols)
    def _():
        loaded(fv, "FV")
        fh[...], fl[...] = halves(fv[...].T)

    @pl.when(in_rows)
    def _():
        loaded(fv, "FV")
        fh[...], fl[...] = halves(fv[...])

    peers = 2 * (R - 1) + Q - 1

    @pl.when(above | below)
    def _():
        pl.semaphore_wait(barrier, peers + 2)

    @pl.when(jnp.logical_not(above | below))
    def _():
        pl.semaphore_wait(barrier, peers)

    for offset, here in ((0, near), (1, above), (-1, below)):
        @pl.when(here)
        def _():
            for j in range(3):
                for k, source in OFFSET.items():
                    if source == offset:
                        push(
                            f_ref.at[j, piece(rows[k]), n_cols], fb.at[j, piece(rows[k])], "FS",
                            rows[k], r * Q + qs[k], j,
                        )
                if offset == 0:
                    push(
                        f_ref.at[j, piece(z), n_cols], fb.at[j, piece(z)], "FS",
                        rows[HR], base + across, j,
                    )

    for k in range(1, Q):
        push(g_ref.at[:, :, span(shares[k], NQ)], gc.at[:, g_rows], "G0", r, base + node[k])
    push(a_ref, abuf.at[:, a_cols], "A", r, base + across, 1)
    push(a_ref, abuf.at[:, a_cols], "A", r, base + sibling, 0)

    def forward(j):
        @pl.when(r != z)
        def _():
            @pl.when(r == partner)
            def _():
                arrived(fb.at[j, : 2 * HZ], "FS", j)

            @pl.when(r != partner)
            def _():
                arrived(fb.at[j, :HZ], "FS", j)

            for k in range(1, R):
                @pl.when(rows[k] != z)
                def _():
                    push(fb.at[j, piece(r)], fb.at[j, piece(r)], "FA", rows[k], base + qs[k], j)

            @pl.when(r == partner)
            def _():
                for k in range(1, R):
                    if k != HR:
                        pltpu.make_async_remote_copy(
                            src_ref=fb.at[j, piece(z)], dst_ref=fb.at[j, piece(z)],
                            send_sem=send.at[BASE["FX"]], recv_sem=recv.at[BASE["FA"] + j],
                            device_id=(rows[k], base + qs[k]), device_id_type=MESH,
                        ).start()

    def g_step(k):
        if k == 0:
            loaded(gc.at[:, g_rows], "LC")
            arrived(gc.at[:, : (Q - 1) * GC], "G0")
        up = gc.at[:, piece(zs[-k % R])]
        down = gc.at[:, piece(zs[k])]
        if k:
            arrived(up, "GP", k - 1)
        push(up, up, "GP", r, zc[1] + q, k)
        if k < R - 1 - HR:
            if k:
                arrived(down, "GM", k - 1)
            push(down, down, "GM", r, zc[R - 1] + q, k)

    def along(k):
        return zd[k % R]

    def product(j):
        @pl.when(r == z)
        def _():
            loaded(fb.at[j], "FB", j)

        @pl.when((r != z) & (r != partner))
        def _():
            arrived(fb.at[j, : (R - 1) * HZ], "FA", j)

        @pl.when(r == partner)
        def _():
            arrived(fb.at[j, : (R - 2) * HZ], "FA", j)

        pb[j] = mm3(ah[...], al[...], fb[j]) * weight(j, z)

        def part(k):
            return pb.at[j, piece(along(k))]

        push(part(4), xb.at[j, 0], "X", r, along(2) * Q + q, j)
        push(part(3), xb.at[j, 1], "X", r, along(1) * Q + q, j)
        push(part(-3), xb.at[j, 2], "X", r, along(-1) * Q + q, j)
        push(part(1), rb.at[j, 0], "RB", r, along(1) * Q + q, j)
        push(part(-1), rb.at[j, 1], "RB", r, along(-1) * Q + q, j)

    def relay(j):
        arrived(xb.at[j], "X", j)
        rl[j, 0] = pb[j, piece(along(2))] + xb[j, 0] + xb[j, 1]
        rl[j, 1] = pb[j, piece(along(-2))] + xb[j, 2]
        push(rl.at[j, 0], rb.at[j, 2], "RB", r, along(2) * Q + q, j)
        push(rl.at[j, 1], rb.at[j, 3], "RB", r, along(-2) * Q + q, j)

    g_step(0)
    forward(0)
    forward(1)
    g_step(1)
    forward(2)
    arrived(abuf.at[:, x_cols], "A", 1)
    push(abuf.at[:, x_cols], abuf.at[:, x_cols], "A", r, base + sibling, 2)
    loaded(abuf.at[:, a_cols], "LA")
    for k in range(1, Q):
        push(g_ref, gn.at[:, n_rows], "GN", r, base + node[k])
        push(d_ref.at[0], db.at[n_rows], "D", r, base + node[k])
    arrived(abuf.at[:, a_cols], "A", 0)
    arrived(abuf.at[:, a_cols], "A", 2)
    ah[...], al[...] = halves(abuf[...])
    product(0)
    g_step(2)
    product(1)
    relay(0)
    product(2)
    relay(1)
    g_step(3)

    def summed(j):
        arrived(rb.at[j], "RB", j)
        return ((pb[j, my_rows] + rb[j, 0]) + (rb[j, 1] + rb[j, 2])) + rb[j, 3]

    def to_unit(j, plane):
        @pl.when(z != plane)
        def _():
            push(yc.at[j], yu.at[my_rows], "YU", r, plane * Q + q, j)

        @pl.when(z == plane)
        def _():
            yu[my_rows] = yc[j]

    yc[0] = -weight(0, r) * summed(0)
    for k in range(1, Q):
        push(yc.at[0], y0n.at[:, n_cols], "Y0", r, base + node[k])
    for plane in planes[:3]:
        to_unit(0, plane)
    y0n[:, n_cols] = yc[0]
    relay(2)
    arrived(y0n.at[:, : (Q - 1) * NQ], "Y0")
    out_ref[0] = y0n[n_rows]
    arrived(gc.at[:, piece(zs[HR])], "GP", HR - 1)
    arrived(gc.at[:, piece(zs[HR - 1])], "GM", HR - 2)
    for j in (1, 2):
        xc[j - 1] = mm(y0n[...], gc[j - 1])

    def child_columns(j):
        yc[j] = -weight(j, r) * (summed(j) + xc[j - 1])
        to_unit(j, planes[2 + j])
        for k in range(1, Q):
            push(
                yc.at[j, span(node[k], GC)], yo.at[j - 1, :, n_cols], "YO", r, base + node[k]
            )
        yo[j - 1, :, n_cols] = yc[j, n_rows]

    def rows_sum(unit, source, place):
        @pl.when(z == planes[unit])
        def _():
            arrived(yu.at[: (R - 1) * HZ], "YU", source)
            tp[...] = mm3(fh[...], fl[...], yu[...]).reshape(R, R, SP, NQ)
            zr[place, 0] = tp[z, r]

            for m in range(R):
                for k in range(R):
                    if m or k:
                        push(
                            tp.at[zs[m], rows[k]], zr.at[place, k], "ZM", rows[k], zc[m] + qs[k], place
                        )

    def cross_sum(unit, child):
        @pl.when(z == planes[unit])
        def _():
            arrived(yu.at[: (R - 1) * HZ], "YU", 0)
            y_hi, y_lo = halves(yu[...].T)
            total = dot(y_hi, fh[...]) + (dot(y_hi, fl[...]) + dot(y_lo, fh[...]))
            tpw[...] = (total * weight(1 + child, r)).reshape(HW, R, SP, W)

            for h in range(HW):
                dest = n * HW + h
                for k in range(R):
                    if k:
                        push(
                            tpw.at[h, rows[k]], wr.at[child, k], "WM", rows[k], dest * Q + qs[k], child
                        )
                        continue

                    @pl.when(dest == z)
                    def _():
                        wr[child, 0] = tpw[h, r]

                    @pl.when(dest != z)
                    def _():
                        push(tpw.at[h, r], wr.at[child, 0], "WM", r, dest * Q + q, child)

    def added(place, plane):
        @pl.when(z == plane)
        def _():
            arrived(zr.at[place, : R - 1], "ZM", place)

        @pl.when(z != plane)
        def _():
            arrived(zr.at[place], "ZM", place)

        return functools.reduce(jnp.add, [zr[place, k] for k in range(R)])

    rows_sum(0, 0, 0)
    cross_sum(1, 0)
    cross_sum(2, 1)
    child_columns(1)
    child_columns(2)
    rows_sum(3, 1, 1)
    rows_sum(4, 2, 2)

    s_rows = span(r, SP)
    zm[...] = added(0, planes[0])
    for k in range(R):
        for w in range(Q):
            if k or w:
                push(zm, zb.at[s_rows, n_cols], "ZB", rows[k], base + node[w])

    zb[s_rows, n_cols] = zm[...]

    holds_w = lax.div(z, HW) == n

    @pl.when(holds_w)
    def _():
        for child in range(2):
            @pl.when(z == planes[1 + child])
            def _():
                arrived(wr.at[child, : R - 1], "WM", child)

            @pl.when(z != planes[1 + child])
            def _():
                arrived(wr.at[child], "WM", child)

            wm[child] = functools.reduce(jnp.add, [wr[child, k] for k in range(R)])

            for k in range(R):
                for w in range(Q):
                    if k or w:
                        share = (shares if k < HR else other_shares)[w]
                        push(
                            wm.at[child, :, span(share, NQ)], wb.at[child, s_rows], "WB",
                            rows[k], base + node[w], child,
                        )

            wb[child, s_rows] = wm[child, :, n_cols]

    loaded(dv, "LD")
    loaded(gn.at[:, n_rows], "LG")
    arrived(gn.at[:, : (Q - 1) * GC], "GN")
    arrived(db.at[: (Q - 1) * GC], "D")
    db[n_rows] = dv[0]
    arrived(fb.at[0, : (C - 1) * SP], "ZB")
    zb[...] = db[...] - zb[...]
    out_ref[3] = zb[n_rows]
    for child in range(2):
        @pl.when(holds_w)
        def _():
            arrived(wb.at[child, : (R - 1) * SP], "WB", child)

        @pl.when(jnp.logical_not(holds_w))
        def _():
            arrived(wb.at[child], "WB", child)

        eb[child] = wb[child] + mm(zb[...], gc[child])
        ge[child] = mm_t(gn[child], eb[child]).reshape(R, R, SP, NQ)
        for k in range(1, R):
            push(ge.at[child, zs[k], r], gz.at[child, R - 1 - k], "GZ", r, zc[k] + q, child)
        for k in range(1, Q):
            push(
                eb.at[child, span(node[k], GC)], uo.at[child, :, n_cols], "UO", r, base + node[k],
            )
        uo[child, :, n_cols] = eb[child, n_rows]

    o_place = lax.div(r, R // Q)
    o_rows = span(r - o_place * (R // Q), SP)
    for child in range(2):
        share = added(1 + child, planes[3 + child])
        arrived(gz.at[child], "GZ", child)
        total = ge[child, z, r] - share
        for k in range(R - 1):
            total = total + gz[child, k]
        zp[child] = total
        for k in range(1, R):
            push(
                zp.at[child], zo.at[child, o_rows, n_cols], "ZO", rows[k], base + o_place, child
            )

        @pl.when(q == o_place)
        def _():
            zo[child, o_rows, n_cols] = zp[child]

        @pl.when(q != o_place)
        def _():
            push(zp.at[child], zo.at[child, o_rows, n_cols], "ZO", r, base + o_place, child)

    arrived(yo.at[:, :, : (Q - 1) * NQ], "YO")
    out_ref[1:3] = yo[...]
    arrived(uo.at[:, :, : (Q - 1) * NQ], "UO")
    out_ref[6:8] = -uo[...]
    for child in range(2):
        @pl.when(q == o_place)
        def _():
            arrived(rb.at[child, 0, : (R - 1) * SP], "ZO", child)

        @pl.when(q != o_place)
        def _():
            arrived(rb.at[child, 0, : R * SP], "ZO", child)

        out_ref[4 + child] = dv[1 + child] + zo[child]

    for k in range(3):
        sent(abuf.at[:, a_cols], "A", k)
    sent(gc.at[:, : (Q - 1) * GC], "G0")
    for k in range(HR):
        sent(gc.at[:, my_rows], "GP", k)
    for k in range(R - 1 - HR):
        sent(gc.at[:, my_rows], "GM", k)
    sent(gn.at[:, : (Q - 1) * GC], "GN")
    sent(db.at[: (Q - 1) * GC], "D")
    sent(y0n.at[:, : (Q - 1) * NQ], "Y0")
    sent(yo.at[:, :, : (Q - 1) * NQ], "YO")
    sent(uo.at[:, :, : (Q - 1) * NQ], "UO")
    sent(fb.at[0, : (C - 1) * SP], "ZB")
    for j in range(3):
        @pl.when(near)
        def _():
            sent(fb.at[j, : 4 * HZ], "FS", j)

        @pl.when(above | below)
        def _():
            sent(fb.at[j, : 2 * HZ], "FS", j)

        @pl.when(r != z)
        def _():
            sent(fb.at[j, : (R - 2) * HZ], "FA", j)

        sent(xb.at[j], "X", j)
        sent(rb.at[j], "RB", j)

    @pl.when(r == partner)
    def _():
        sent(fb.at[:, : (R - 2) * HZ], "FX")

    for j in range(3):
        targets = planes[:3] if j == 0 else planes[2 + j : 3 + j]
        inside = functools.reduce(jnp.logical_or, [z == plane for plane in targets])

        @pl.when(inside)
        def _():
            if len(targets) > 1:
                sent(yu.at[: (len(targets) - 1) * HZ], "YU", j)

        @pl.when(jnp.logical_not(inside))
        def _():
            sent(yu.at[: len(targets) * HZ], "YU", j)

    for unit, place in ((0, 0), (3, 1), (4, 2)):
        @pl.when(z == planes[unit])
        def _():
            sent(fb.at[0, : (R * R - 1) * SP], "ZM", place)

    for child in range(2):
        @pl.when((z == planes[1 + child]) & holds_w)
        def _():
            sent(fv.at[: (R * HW - 1) * SP], "WM", child)

        @pl.when((z == planes[1 + child]) & jnp.logical_not(holds_w))
        def _():
            sent(fv.at[: R * HW * SP], "WM", child)

    for child in range(2):
        @pl.when(holds_w)
        def _():
            sent(fb.at[0, : (C - 1) * SP], "WB", child)

        sent(gz.at[child], "GZ", child)

        @pl.when(q == o_place)
        def _():
            sent(rb.at[child, 0, : (R - 1) * SP], "ZO", child)

        @pl.when(q != o_place)
        def _():
            sent(rb.at[child, 0, : R * SP], "ZO", child)


def shards(region_inverse, factor_cols, parent_factor, diag_inverse, listed):
    R = lax.axis_size("row")
    C = lax.axis_size("col")
    W = factor_cols.shape[2]
    Q = C // R
    NQ, HZ, GC = W // Q, W // R, W // C
    SP = HZ // R
    HW = NQ // HZ
    planes = (0, 2, 5, 3, 7)
    f32 = jnp.float32
    vmem = pl.BlockSpec(memory_space=pltpu.VMEM)
    smem = pl.BlockSpec(memory_space=pltpu.SMEM)
    scratch = [
        (W, W), (3, W, NQ), (W, W), (3, W, NQ), (3, 3, HZ, NQ), (3, 2, HZ, NQ), (3, 4, HZ, NQ),
        (2, W, NQ), (2, HZ, W), (HZ, W), (3, GC, W), (HZ, W), (3, HZ, NQ), (2, HZ, NQ), (2, GC, W),
        (W, NQ), (R, R, SP, NQ), (HW, R, SP, W), (3, R, SP, NQ), (2, R, SP, W),
        (SP, NQ), (HZ, W), (2, SP, W), (2, HZ, NQ), (2, HZ, NQ), (2, GC, W),
        (2, R, R, SP, NQ), (2, R - 1, SP, NQ), (2, SP, NQ), (2, GC, W),
    ]
    hbm = pl.BlockSpec(memory_space=pl.ANY)
    whole = pl.pallas_call(
        functools.partial(kernel, R, C, W, planes),
        out_shape=jax.ShapeDtypeStruct((8, GC, W), f32),
        in_specs=[hbm, hbm, hbm, hbm, smem],
        out_specs=vmem,
        scratch_shapes=[pltpu.VMEM(shape, f32) for shape in scratch]
        + [pltpu.VMEM((W, W), jnp.bfloat16)] * 4
        + [pltpu.SemaphoreType.DMA((N_SEM,)), pltpu.SemaphoreType.DMA((N_SEM,))],
        compiler_params=pltpu.CompilerParams(
            collective_id=0, has_side_effects=True, vmem_limit_bytes=60 * 2**20
        ),
    )(region_inverse, factor_cols, parent_factor, diag_inverse, listed)
    return pl.pallas_call(
        split,
        out_shape=(
            jax.ShapeDtypeStruct((3, GC, W), f32),
            jax.ShapeDtypeStruct((3, GC, W), f32),
            jax.ShapeDtypeStruct((2, GC, W), f32),
        ),
        in_specs=[vmem],
        out_specs=(vmem, vmem, vmem),
        compiler_params=pltpu.CompilerParams(vmem_limit_bytes=4 * 2**20),
    )(whole)


def split(whole_ref, col_ref, diag_ref, par_ref):
    col_ref[...] = whole_ref[0:3]
    diag_ref[...] = whole_ref[3:6]
    par_ref[...] = whole_ref[6:8]


def solution(mesh):
    in_specs = (
        P("row", "col"),
        P(None, "row", None),
        P(None, "col", None),
        P(None, "col", None),
        P(),
    )
    out_specs = (P(None, ("row", "col"), None), P(None, "col", None), P(None, "col", None))
    return jax.shard_map(shards, mesh=mesh, in_specs=in_specs, out_specs=out_specs, check_vma=False)
```

```python
import functools

import jax
import jax.numpy as jnp
from jax import lax
from jax.experimental import pallas as pl
from jax.experimental.pallas import tpu as pltpu
from jax.sharding import PartitionSpec as P

MESH = pl.DeviceIdType.MESH
HIGH = lax.Precision.HIGHEST

SIZES = dict(
    A=3, FS=3, FA=3, FX=1, GN=1, G0=1, D=1, GP=4, GM=3, X=3, RB=3, Y0=1, YO=1, YU=3, ZM=3, ZB=1, WM=2,
    WB=2, UO=1, GZ=2, ZO=2, FB=3, FV=1, LA=1, LG=1, LC=1, LD=1,
)
BASE = {}
N_SEM = 0
for _name, _size in SIZES.items():
    BASE[_name] = N_SEM
    N_SEM += _size

def halves(x):
    hi = x.astype(jnp.bfloat16)
    return hi, (x - hi.astype(jnp.float32)).astype(jnp.bfloat16)


def dot(a, b, dims=((1,), (0,))):
    return lax.dot_general(a, b, (dims, ((), ())), preferred_element_type=jnp.float32)


def mm3(a_hi, a_lo, b):
    b_hi, b_lo = halves(b)
    cols = b.shape[1]
    both = dot(a_hi, jnp.concatenate([b_hi, b_lo], axis=1))
    return both[:, :cols] + (both[:, cols:] + dot(a_lo, b_hi))


def mm(a, b):
    return mm3(*halves(a), b)


def mm_t(a, b):
    return lax.dot_general(
        a, b, (((0,), (0,)), ((), ())), precision=HIGH, preferred_element_type=jnp.float32
    )


def kernel(
    R, C, W, planes,
    a_ref, f_ref, g_ref, d_ref, listed_ref,
    out_ref,
    abuf, fb, fv, pb, xb, rl, rb, gc, gn, db, dv, y0n, yc, xc, yo, yu, tp, tpw, zr, wr,
    zm, zb, wm, wb, eb, uo, ge, gz, zp, zo, ah, al, fh, fl, send, recv,
):
    Q = C // R
    NQ, HZ, GC = W // Q, W // R, W // C
    SP = HZ // R
    HW = NQ // HZ
    HR = R // 2
    r = lax.axis_index("row")
    c = lax.axis_index("col")

    def wrap(value, size):
        return jnp.where(value >= size, value - size, value)

    z = lax.div(c, Q)
    q = c - z * Q
    half = lax.div(r, HR)
    y = r - half * HR
    pair = lax.div(q, 2)
    core = q - pair * 2
    z_half = lax.div(z, HR)
    kind = jnp.where(pair == half, 0, 1)
    across = 2 * (1 - pair) + core
    sibling = 2 * pair + 1 - core
    diagonal = 2 * (1 - pair) + 1 - core
    node = (q, sibling, across, diagonal)
    n = 2 * kind + core
    shares = (n, 2 * kind + 1 - core, 2 * (1 - kind) + core, 2 * (1 - kind) + 1 - core)
    other_shares = (shares[2], shares[3], shares[0], shares[1])
    ys = [wrap(y + k, HR) if k else y for k in range(HR)]
    rows = [half * HR + v for v in ys] + [(1 - half) * HR + v for v in ys]
    qs = [q] * HR + [across] * HR
    zs = [wrap(z + k, R) if k else z for k in range(R)]
    zc = [v * Q for v in zs]
    base = zc[0]
    zd = [zs[k] if k % HR == 0 else jnp.where(core == 0, zs[k], zs[R - k]) for k in range(R)]
    partner = z + HR - 2 * HR * z_half

    def span(i, size):
        return pl.ds(pl.multiple_of(i * size, size), size)

    def piece(i):
        return span(i, HZ)

    n_cols = span(n, NQ)
    my_rows = piece(z)

    def push(src, dst, s, row, col, k=0):
        s = BASE[s] + k
        pltpu.make_async_remote_copy(
            src_ref=src, dst_ref=dst, send_sem=send.at[s], recv_sem=recv.at[s],
            device_id=(row, col), device_id_type=MESH,
        ).start()

    def arrived(view, s, k=0):
        pltpu.make_async_copy(view, view, recv.at[BASE[s] + k]).wait()

    def sent(view, s, k=0):
        pltpu.make_async_copy(view, view, send.at[BASE[s] + k]).wait()

    def weight(member, block):
        return listed_ref[member, block].astype(jnp.float32)

    barrier = pltpu.get_barrier_semaphore()

    def greet(row, col):
        pl.semaphore_signal(barrier, inc=1, device_id=(row, col), device_id_type=MESH)

    for k in range(1, R):
        greet(rows[k], base + qs[k])
    for k in range(1, R):
        greet(r, zc[k] + q)
    for k in range(1, Q):
        greet(r, base + node[k])
    near = z == r
    a_cols = span(q, NQ)
    x_cols = span(across, NQ)
    n_rows = span(q, GC)
    g_rows = span(c, GC)

    def local(src, dst, s, k=0):
        pltpu.make_async_copy(src, dst, recv.at[BASE[s] + k]).start()

    def loaded(view, s, k=0):
        pltpu.make_async_copy(view, view, recv.at[BASE[s] + k]).wait()

    @pl.when(near)
    def _():
        for j in range(3):
            local(f_ref.at[j, :, n_cols], fb.at[j], "FB", j)

    local(a_ref, abuf.at[:, a_cols], "LA")
    local(g_ref.at[:, :, n_cols], gc.at[:, g_rows], "LC")
    for unit, member in enumerate((0, 1, 2, 1, 2)):
        @pl.when(z == planes[unit])
        def _():
            local(f_ref.at[member], fv, "FV")


    local(g_ref, gn.at[:, n_rows], "LG")
    local(d_ref, dv, "LD")
    in_cols = functools.reduce(jnp.logical_or, [z == planes[unit] for unit in (0, 3, 4)])
    in_rows = functools.reduce(jnp.logical_or, [z == planes[unit] for unit in (1, 2)])

    @pl.when(in_cols)
    def _():
        loaded(fv, "FV")
        fh[...], fl[...] = halves(fv[...].T)

    @pl.when(in_rows)
    def _():
        loaded(fv, "FV")
        fh[...], fl[...] = halves(fv[...])

    pl.semaphore_wait(barrier, 2 * (R - 1) + Q - 1)

    @pl.when(near)
    def _():
        for j in range(3):
            loaded(fb.at[j], "FB", j)
            for k in range(1, R):
                push(
                    fb.at[j, piece(rows[k])], fb.at[j, piece(rows[k])], "FS", rows[k], base + qs[k], j
                )
            push(fb.at[j, piece(z)], fb.at[j, piece(z)], "FS", rows[HR], base + across, j)

    for k in range(1, Q):
        push(g_ref.at[:, :, span(shares[k], NQ)], gc.at[:, g_rows], "G0", r, base + node[k])
    loaded(abuf.at[:, a_cols], "LA")
    push(abuf.at[:, a_cols], abuf.at[:, a_cols], "A", r, base + across, 1)
    push(abuf.at[:, a_cols], abuf.at[:, a_cols], "A", r, base + sibling, 0)

    def forward(j):
        @pl.when(r != z)
        def _():
            @pl.when(r == partner)
            def _():
                arrived(fb.at[j, : 2 * HZ], "FS", j)

            @pl.when(r != partner)
            def _():
                arrived(fb.at[j, :HZ], "FS", j)

            for k in range(1, R):
                @pl.when(rows[k] != z)
                def _():
                    push(fb.at[j, piece(r)], fb.at[j, piece(r)], "FA", rows[k], base + qs[k], j)

            @pl.when(r == partner)
            def _():
                for k in range(1, R):
                    if k != HR:
                        pltpu.make_async_remote_copy(
                            src_ref=fb.at[j, piece(z)], dst_ref=fb.at[j, piece(z)],
                            send_sem=send.at[BASE["FX"]], recv_sem=recv.at[BASE["FA"] + j],
                            device_id=(rows[k], base + qs[k]), device_id_type=MESH,
                        ).start()

    def g_step(k):
        if k == 0:
            loaded(gc.at[:, g_rows], "LC")
            arrived(gc.at[:, : (Q - 1) * GC], "G0")
        up = gc.at[:, piece(zs[-k % R])]
        down = gc.at[:, piece(zs[k])]
        if k:
            arrived(up, "GP", k - 1)
        push(up, up, "GP", r, zc[1] + q, k)
        if k < R - 1 - HR:
            if k:
                arrived(down, "GM", k - 1)
            push(down, down, "GM", r, zc[R - 1] + q, k)

    def along(k):
        return zd[k % R]

    def product(j):
        @pl.when((r != z) & (r != partner))
        def _():
            arrived(fb.at[j, : (R - 1) * HZ], "FA", j)

        @pl.when(r == partner)
        def _():
            arrived(fb.at[j, : (R - 2) * HZ], "FA", j)

        pb[j] = mm3(ah[...], al[...], fb[j]) * weight(j, z)

        def part(k):
            return pb.at[j, piece(along(k))]

        push(part(4), xb.at[j, 0], "X", r, along(2) * Q + q, j)
        push(part(3), xb.at[j, 1], "X", r, along(1) * Q + q, j)
        push(part(-3), xb.at[j, 2], "X", r, along(-1) * Q + q, j)
        push(part(1), rb.at[j, 0], "RB", r, along(1) * Q + q, j)
        push(part(-1), rb.at[j, 1], "RB", r, along(-1) * Q + q, j)

    def relay(j):
        arrived(xb.at[j], "X", j)
        rl[j, 0] = pb[j, piece(along(2))] + xb[j, 0] + xb[j, 1]
        rl[j, 1] = pb[j, piece(along(-2))] + xb[j, 2]
        push(rl.at[j, 0], rb.at[j, 2], "RB", r, along(2) * Q + q, j)
        push(rl.at[j, 1], rb.at[j, 3], "RB", r, along(-2) * Q + q, j)

    g_step(0)
    forward(0)
    forward(1)
    g_step(1)
    forward(2)
    arrived(abuf.at[:, x_cols], "A", 1)
    push(abuf.at[:, x_cols], abuf.at[:, x_cols], "A", r, base + sibling, 2)
    for k in range(1, Q):
        push(g_ref, gn.at[:, n_rows], "GN", r, base + node[k])
        push(d_ref.at[0], db.at[n_rows], "D", r, base + node[k])
    arrived(abuf.at[:, a_cols], "A", 0)
    arrived(abuf.at[:, a_cols], "A", 2)
    ah[...], al[...] = halves(abuf[...])
    product(0)
    g_step(2)
    product(1)
    relay(0)
    product(2)
    relay(1)
    g_step(3)

    def summed(j):
        arrived(rb.at[j], "RB", j)
        return ((pb[j, my_rows] + rb[j, 0]) + (rb[j, 1] + rb[j, 2])) + rb[j, 3]

    def to_unit(j, plane):
        @pl.when(z != plane)
        def _():
            push(yc.at[j], yu.at[my_rows], "YU", r, plane * Q + q, j)

        @pl.when(z == plane)
        def _():
            yu[my_rows] = yc[j]

    yc[0] = -weight(0, r) * summed(0)
    for k in range(1, Q):
        push(yc.at[0], y0n.at[:, n_cols], "Y0", r, base + node[k])
    for plane in planes[:3]:
        to_unit(0, plane)
    y0n[:, n_cols] = yc[0]
    relay(2)
    arrived(y0n.at[:, : (Q - 1) * NQ], "Y0")
    out_ref[0] = y0n[n_rows]
    arrived(gc.at[:, piece(zs[HR])], "GP", HR - 1)
    arrived(gc.at[:, piece(zs[HR - 1])], "GM", HR - 2)
    for j in (1, 2):
        xc[j - 1] = mm(y0n[...], gc[j - 1])

    def child_columns(j):
        yc[j] = -weight(j, r) * (summed(j) + xc[j - 1])
        to_unit(j, planes[2 + j])
        for k in range(1, Q):
            push(
                yc.at[j, span(node[k], GC)], yo.at[j - 1, :, n_cols], "YO", r, base + node[k]
            )
        yo[j - 1, :, n_cols] = yc[j, n_rows]

    def rows_sum(unit, source, place):
        @pl.when(z == planes[unit])
        def _():
            arrived(yu.at[: (R - 1) * HZ], "YU", source)
            tp[...] = mm3(fh[...], fl[...], yu[...]).reshape(R, R, SP, NQ)
            zr[place, 0] = tp[z, r]

            for m in range(R):
                for k in range(R):
                    if m or k:
                        push(
                            tp.at[zs[m], rows[k]], zr.at[place, k], "ZM", rows[k], zc[m] + qs[k], place
                        )

    def cross_sum(unit, child):
        @pl.when(z == planes[unit])
        def _():
            arrived(yu.at[: (R - 1) * HZ], "YU", 0)
            y_hi, y_lo = halves(yu[...].T)
            total = dot(y_hi, fh[...]) + (dot(y_hi, fl[...]) + dot(y_lo, fh[...]))
            tpw[...] = (total * weight(1 + child, r)).reshape(HW, R, SP, W)

            for h in range(HW):
                dest = n * HW + h
                for k in range(R):
                    if k:
                        push(
                            tpw.at[h, rows[k]], wr.at[child, k], "WM", rows[k], dest * Q + qs[k], child
                        )
                        continue

                    @pl.when(dest == z)
                    def _():
                        wr[child, 0] = tpw[h, r]

                    @pl.when(dest != z)
                    def _():
                        push(tpw.at[h, r], wr.at[child, 0], "WM", r, dest * Q + q, child)

    def added(place, plane):
        @pl.when(z == plane)
        def _():
            arrived(zr.at[place, : R - 1], "ZM", place)

        @pl.when(z != plane)
        def _():
            arrived(zr.at[place], "ZM", place)

        return functools.reduce(jnp.add, [zr[place, k] for k in range(R)])

    rows_sum(0, 0, 0)
    cross_sum(1, 0)
    cross_sum(2, 1)
    child_columns(1)
    child_columns(2)
    rows_sum(3, 1, 1)
    rows_sum(4, 2, 2)

    s_rows = span(r, SP)
    zm[...] = added(0, planes[0])
    for k in range(R):
        for w in range(Q):
            if k or w:
                push(zm, zb.at[s_rows, n_cols], "ZB", rows[k], base + node[w])

    zb[s_rows, n_cols] = zm[...]

    holds_w = lax.div(z, HW) == n

    @pl.when(holds_w)
    def _():
        for child in range(2):
            @pl.when(z == planes[1 + child])
            def _():
                arrived(wr.at[child, : R - 1], "WM", child)

            @pl.when(z != planes[1 + child])
            def _():
                arrived(wr.at[child], "WM", child)

            wm[child] = functools.reduce(jnp.add, [wr[child, k] for k in range(R)])

            for k in range(R):
                for w in range(Q):
                    if k or w:
                        share = (shares if k < HR else other_shares)[w]
                        push(
                            wm.at[child, :, span(share, NQ)], wb.at[child, s_rows], "WB",
                            rows[k], base + node[w], child,
                        )

            wb[child, s_rows] = wm[child, :, n_cols]

    loaded(dv, "LD")
    loaded(gn.at[:, n_rows], "LG")
    arrived(gn.at[:, : (Q - 1) * GC], "GN")
    arrived(db.at[: (Q - 1) * GC], "D")
    db[n_rows] = dv[0]
    arrived(fb.at[0, : (C - 1) * SP], "ZB")
    zb[...] = db[...] - zb[...]
    out_ref[3] = zb[n_rows]
    for child in range(2):
        @pl.when(holds_w)
        def _():
            arrived(wb.at[child, : (R - 1) * SP], "WB", child)

        @pl.when(jnp.logical_not(holds_w))
        def _():
            arrived(wb.at[child], "WB", child)

        eb[child] = wb[child] + mm(zb[...], gc[child])
        ge[child] = mm_t(gn[child], eb[child]).reshape(R, R, SP, NQ)
        for k in range(1, R):
            push(ge.at[child, zs[k], r], gz.at[child, R - 1 - k], "GZ", r, zc[k] + q, child)
        for k in range(1, Q):
            push(
                eb.at[child, span(node[k], GC)], uo.at[child, :, n_cols], "UO", r, base + node[k],
            )
        uo[child, :, n_cols] = eb[child, n_rows]

    o_place = lax.div(r, R // Q)
    o_rows = span(r - o_place * (R // Q), SP)
    for child in range(2):
        share = added(1 + child, planes[3 + child])
        arrived(gz.at[child], "GZ", child)
        total = ge[child, z, r] - share
        for k in range(R - 1):
            total = total + gz[child, k]
        zp[child] = total
        for k in range(1, R):
            push(
                zp.at[child], zo.at[child, o_rows, n_cols], "ZO", rows[k], base + o_place, child
            )

        @pl.when(q == o_place)
        def _():
            zo[child, o_rows, n_cols] = zp[child]

        @pl.when(q != o_place)
        def _():
            push(zp.at[child], zo.at[child, o_rows, n_cols], "ZO", r, base + o_place, child)

    arrived(yo.at[:, :, : (Q - 1) * NQ], "YO")
    out_ref[1:3] = yo[...]
    arrived(uo.at[:, :, : (Q - 1) * NQ], "UO")
    out_ref[6:8] = -uo[...]
    for child in range(2):
        @pl.when(q == o_place)
        def _():
            arrived(rb.at[child, 0, : (R - 1) * SP], "ZO", child)

        @pl.when(q != o_place)
        def _():
            arrived(rb.at[child, 0, : R * SP], "ZO", child)

        out_ref[4 + child] = dv[1 + child] + zo[child]

    for k in range(3):
        sent(abuf.at[:, a_cols], "A", k)
    sent(gc.at[:, : (Q - 1) * GC], "G0")
    for k in range(HR):
        sent(gc.at[:, my_rows], "GP", k)
    for k in range(R - 1 - HR):
        sent(gc.at[:, my_rows], "GM", k)
    sent(gn.at[:, : (Q - 1) * GC], "GN")
    sent(db.at[: (Q - 1) * GC], "D")
    sent(y0n.at[:, : (Q - 1) * NQ], "Y0")
    sent(yo.at[:, :, : (Q - 1) * NQ], "YO")
    sent(uo.at[:, :, : (Q - 1) * NQ], "UO")
    sent(fb.at[0, : (C - 1) * SP], "ZB")
    for j in range(3):
        @pl.when(near)
        def _():
            sent(fb.at[j], "FS", j)

        @pl.when(r != z)
        def _():
            sent(fb.at[j, : (R - 2) * HZ], "FA", j)

        sent(xb.at[j], "X", j)
        sent(rb.at[j], "RB", j)

    @pl.when(r == partner)
    def _():
        sent(fb.at[:, : (R - 2) * HZ], "FX")

    for j in range(3):
        targets = planes[:3] if j == 0 else planes[2 + j : 3 + j]
        inside = functools.reduce(jnp.logical_or, [z == plane for plane in targets])

        @pl.when(inside)
        def _():
            if len(targets) > 1:
                sent(yu.at[: (len(targets) - 1) * HZ], "YU", j)

        @pl.when(jnp.logical_not(inside))
        def _():
            sent(yu.at[: len(targets) * HZ], "YU", j)

    for unit, place in ((0, 0), (3, 1), (4, 2)):
        @pl.when(z == planes[unit])
        def _():
            sent(fb.at[0, : (R * R - 1) * SP], "ZM", place)

    for child in range(2):
        @pl.when((z == planes[1 + child]) & holds_w)
        def _():
            sent(fv.at[: (R * HW - 1) * SP], "WM", child)

        @pl.when((z == planes[1 + child]) & jnp.logical_not(holds_w))
        def _():
            sent(fv.at[: R * HW * SP], "WM", child)

    for child in range(2):
        @pl.when(holds_w)
        def _():
            sent(fb.at[0, : (C - 1) * SP], "WB", child)

        sent(gz.at[child], "GZ", child)

        @pl.when(q == o_place)
        def _():
            sent(rb.at[child, 0, : (R - 1) * SP], "ZO", child)

        @pl.when(q != o_place)
        def _():
            sent(rb.at[child, 0, : R * SP], "ZO", child)


def shards(region_inverse, factor_cols, parent_factor, diag_inverse, listed):
    R = lax.axis_size("row")
    C = lax.axis_size("col")
    W = factor_cols.shape[2]
    Q = C // R
    NQ, HZ, GC = W // Q, W // R, W // C
    SP = HZ // R
    HW = NQ // HZ
    planes = (0, 2, 5, 3, 7)
    f32 = jnp.float32
    vmem = pl.BlockSpec(memory_space=pltpu.VMEM)
    smem = pl.BlockSpec(memory_space=pltpu.SMEM)
    scratch = [
        (W, W), (3, W, NQ), (W, W), (3, W, NQ), (3, 3, HZ, NQ), (3, 2, HZ, NQ), (3, 4, HZ, NQ),
        (2, W, NQ), (2, HZ, W), (HZ, W), (3, GC, W), (HZ, W), (3, HZ, NQ), (2, HZ, NQ), (2, GC, W),
        (W, NQ), (R, R, SP, NQ), (HW, R, SP, W), (3, R, SP, NQ), (2, R, SP, W),
        (SP, NQ), (HZ, W), (2, SP, W), (2, HZ, NQ), (2, HZ, NQ), (2, GC, W),
        (2, R, R, SP, NQ), (2, R - 1, SP, NQ), (2, SP, NQ), (2, GC, W),
    ]
    hbm = pl.BlockSpec(memory_space=pl.ANY)
    whole = pl.pallas_call(
        functools.partial(kernel, R, C, W, planes),
        out_shape=jax.ShapeDtypeStruct((8, GC, W), f32),
        in_specs=[hbm, hbm, hbm, hbm, smem],
        out_specs=vmem,
        scratch_shapes=[pltpu.VMEM(shape, f32) for shape in scratch]
        + [pltpu.VMEM((W, W), jnp.bfloat16)] * 4
        + [pltpu.SemaphoreType.DMA((N_SEM,)), pltpu.SemaphoreType.DMA((N_SEM,))],
        compiler_params=pltpu.CompilerParams(
            collective_id=0, has_side_effects=True, vmem_limit_bytes=60 * 2**20
        ),
    )(region_inverse, factor_cols, parent_factor, diag_inverse, listed)
    return pl.pallas_call(
        split,
        out_shape=(
            jax.ShapeDtypeStruct((3, GC, W), f32),
            jax.ShapeDtypeStruct((3, GC, W), f32),
            jax.ShapeDtypeStruct((2, GC, W), f32),
        ),
        in_specs=[vmem],
        out_specs=(vmem, vmem, vmem),
        compiler_params=pltpu.CompilerParams(vmem_limit_bytes=4 * 2**20),
    )(whole)


def split(whole_ref, col_ref, diag_ref, par_ref):
    col_ref[...] = whole_ref[0:3]
    diag_ref[...] = whole_ref[3:6]
    par_ref[...] = whole_ref[6:8]


def solution(mesh):
    in_specs = (
        P("row", "col"),
        P(None, "row", None),
        P(None, "col", None),
        P(None, "col", None),
        P(),
    )
    out_specs = (P(None, ("row", "col"), None), P(None, "col", None), P(None, "col", None))
    return jax.shard_map(shards, mesh=mesh, in_specs=in_specs, out_specs=out_specs, check_vma=False)
```

```python
import functools

import jax
import jax.numpy as jnp
from jax import lax
from jax.experimental import pallas as pl
from jax.experimental.pallas import tpu as pltpu
from jax.sharding import PartitionSpec as P

MESH = pl.DeviceIdType.MESH
HIGH = lax.Precision.HIGHEST

SIZES = dict(
    A=3, FS=3, FA=3, FX=1, GN=1, G0=1, D=1, GP=1, X=3, RB=3, Y0=1, YO=1, YU=3, ZM=3, ZB=1, WM=2,
    WB=2, UO=1, GZ=2, ZO=2, FB=3, FV=1, LA=1, LG=1, LC=1, LD=1,
)
BASE = {}
N_SEM = 0
for _name, _size in SIZES.items():
    BASE[_name] = N_SEM
    N_SEM += _size

def halves(x):
    hi = x.astype(jnp.bfloat16)
    return hi, (x - hi.astype(jnp.float32)).astype(jnp.bfloat16)


def dot(a, b, dims=((1,), (0,))):
    return lax.dot_general(a, b, (dims, ((), ())), preferred_element_type=jnp.float32)


def mm3(a_hi, a_lo, b):
    b_hi, b_lo = halves(b)
    cols = b.shape[1]
    both = dot(a_hi, jnp.concatenate([b_hi, b_lo], axis=1))
    return both[:, :cols] + (both[:, cols:] + dot(a_lo, b_hi))


def mm(a, b):
    return mm3(*halves(a), b)


def mm_t(a, b):
    return lax.dot_general(
        a, b, (((0,), (0,)), ((), ())), precision=HIGH, preferred_element_type=jnp.float32
    )


def kernel(
    R, C, W, planes,
    a_ref, f_ref, g_ref, d_ref, listed_ref,
    out_ref,
    abuf, fb, fv, pb, xb, rl, rb, gc, gn, db, dv, y0n, yc, xc, yo, yu, tp, tpw, zr, wr,
    zm, zb, wm, wb, eb, uo, ge, gz, zp, zo, ah, al, fh, fl, send, recv,
):
    Q = C // R
    NQ, HZ, GC = W // Q, W // R, W // C
    SP = HZ // R
    HW = NQ // HZ
    HR = R // 2
    r = lax.axis_index("row")
    c = lax.axis_index("col")

    def wrap(value, size):
        return jnp.where(value >= size, value - size, value)

    z = lax.div(c, Q)
    q = c - z * Q
    half = lax.div(r, HR)
    y = r - half * HR
    pair = lax.div(q, 2)
    core = q - pair * 2
    z_half = lax.div(z, HR)
    kind = jnp.where(pair == half, 0, 1)
    across = 2 * (1 - pair) + core
    sibling = 2 * pair + 1 - core
    diagonal = 2 * (1 - pair) + 1 - core
    node = (q, sibling, across, diagonal)
    n = 2 * kind + core
    shares = (n, 2 * kind + 1 - core, 2 * (1 - kind) + core, 2 * (1 - kind) + 1 - core)
    other_shares = (shares[2], shares[3], shares[0], shares[1])
    ys = [wrap(y + k, HR) if k else y for k in range(HR)]
    rows = [half * HR + v for v in ys] + [(1 - half) * HR + v for v in ys]
    qs = [q] * HR + [across] * HR
    zs = [wrap(z + k, R) if k else z for k in range(R)]
    zc = [v * Q for v in zs]
    base = zc[0]
    zd = [zs[k] if k % HR == 0 else jnp.where(core == 0, zs[k], zs[R - k]) for k in range(R)]
    partner = z + HR - 2 * HR * z_half

    def span(i, size):
        return pl.ds(pl.multiple_of(i * size, size), size)

    def piece(i):
        return span(i, HZ)

    n_cols = span(n, NQ)
    my_rows = piece(z)

    def push(src, dst, s, row, col, k=0):
        s = BASE[s] + k
        pltpu.make_async_remote_copy(
            src_ref=src, dst_ref=dst, send_sem=send.at[s], recv_sem=recv.at[s],
            device_id=(row, col), device_id_type=MESH,
        ).start()

    def arrived(view, s, k=0):
        pltpu.make_async_copy(view, view, recv.at[BASE[s] + k]).wait()

    def sent(view, s, k=0):
        pltpu.make_async_copy(view, view, send.at[BASE[s] + k]).wait()

    def weight(member, block):
        return listed_ref[member, block].astype(jnp.float32)

    barrier = pltpu.get_barrier_semaphore()

    def greet(row, col):
        pl.semaphore_signal(barrier, inc=1, device_id=(row, col), device_id_type=MESH)

    for k in range(1, R):
        greet(rows[k], base + qs[k])
    for k in range(1, R):
        greet(r, zc[k] + q)
    for k in range(1, Q):
        greet(r, base + node[k])
    near = z == r
    a_cols = span(q, NQ)
    x_cols = span(across, NQ)
    n_rows = span(q, GC)
    g_rows = span(c, GC)

    def local(src, dst, s, k=0):
        pltpu.make_async_copy(src, dst, recv.at[BASE[s] + k]).start()

    def loaded(view, s, k=0):
        pltpu.make_async_copy(view, view, recv.at[BASE[s] + k]).wait()

    @pl.when(near)
    def _():
        for j in range(3):
            local(f_ref.at[j, :, n_cols], fb.at[j], "FB", j)

    local(a_ref, abuf.at[:, a_cols], "LA")
    local(g_ref.at[:, :, n_cols], gc.at[:, g_rows], "LC")
    for unit, member in enumerate((0, 1, 2, 1, 2)):
        @pl.when(z == planes[unit])
        def _():
            local(f_ref.at[member], fv, "FV")


    local(g_ref, gn.at[:, n_rows], "LG")
    local(d_ref, dv, "LD")
    in_cols = functools.reduce(jnp.logical_or, [z == planes[unit] for unit in (0, 3, 4)])
    in_rows = functools.reduce(jnp.logical_or, [z == planes[unit] for unit in (1, 2)])

    @pl.when(in_cols)
    def _():
        loaded(fv, "FV")
        fh[...], fl[...] = halves(fv[...].T)

    @pl.when(in_rows)
    def _():
        loaded(fv, "FV")
        fh[...], fl[...] = halves(fv[...])

    pl.semaphore_wait(barrier, 2 * (R - 1) + Q - 1)

    @pl.when(near)
    def _():
        for j in range(3):
            loaded(fb.at[j], "FB", j)
            for k in range(1, R):
                push(
                    fb.at[j, piece(rows[k])], fb.at[j, piece(rows[k])], "FS", rows[k], base + qs[k], j
                )
            push(fb.at[j, piece(z)], fb.at[j, piece(z)], "FS", rows[HR], base + across, j)
            for k in range(1, HR):
                push(fb.at[j, piece(z)], fb.at[j, piece(z)], "FA", rows[k], base + q, j)

    for k in range(1, Q):
        push(g_ref.at[:, :, span(shares[k], NQ)], gc.at[:, g_rows], "G0", r, base + node[k])
    loaded(abuf.at[:, a_cols], "LA")
    push(abuf.at[:, a_cols], abuf.at[:, a_cols], "A", r, base + across, 1)
    push(abuf.at[:, a_cols], abuf.at[:, a_cols], "A", r, base + sibling, 0)

    def forward(j):
        @pl.when(r != z)
        def _():
            @pl.when(r == partner)
            def _():
                arrived(fb.at[j, : 2 * HZ], "FS", j)

            @pl.when(r != partner)
            def _():
                arrived(fb.at[j, :HZ], "FS", j)

            for k in range(1, R):
                @pl.when(rows[k] != z)
                def _():
                    push(fb.at[j, piece(r)], fb.at[j, piece(r)], "FA", rows[k], base + qs[k], j)

            @pl.when(r == partner)
            def _():
                for k in range(1, HR):
                    pltpu.make_async_remote_copy(
                        src_ref=fb.at[j, piece(z)], dst_ref=fb.at[j, piece(z)],
                        send_sem=send.at[BASE["FX"]], recv_sem=recv.at[BASE["FA"] + j],
                        device_id=(rows[k], base + q), device_id_type=MESH,
                    ).start()

    def share_columns():
        loaded(gc.at[:, g_rows], "LC")
        arrived(gc.at[:, : (Q - 1) * GC], "G0")
        for k in range(1, R):
            push(gc.at[:, my_rows], gc.at[:, my_rows], "GP", r, zc[k] + q)

    def along(k):
        return zd[k % R]

    def product(j):
        @pl.when((r != z) & (r != partner))
        def _():
            arrived(fb.at[j, : (R - 1) * HZ], "FA", j)

        @pl.when(r == partner)
        def _():
            arrived(fb.at[j, : (R - 2) * HZ], "FA", j)

        pb[j] = mm3(ah[...], al[...], fb[j]) * weight(j, z)

        def part(k):
            return pb.at[j, piece(along(k))]

        push(part(4), xb.at[j, 0], "X", r, along(2) * Q + q, j)
        push(part(3), xb.at[j, 1], "X", r, along(1) * Q + q, j)
        push(part(-3), xb.at[j, 2], "X", r, along(-1) * Q + q, j)
        push(part(1), rb.at[j, 0], "RB", r, along(1) * Q + q, j)
        push(part(-1), rb.at[j, 1], "RB", r, along(-1) * Q + q, j)

    def relay(j):
        arrived(xb.at[j], "X", j)
        rl[j, 0] = pb[j, piece(along(2))] + xb[j, 0] + xb[j, 1]
        rl[j, 1] = pb[j, piece(along(-2))] + xb[j, 2]
        push(rl.at[j, 0], rb.at[j, 2], "RB", r, along(2) * Q + q, j)
        push(rl.at[j, 1], rb.at[j, 3], "RB", r, along(-2) * Q + q, j)

    share_columns()
    forward(0)
    forward(1)
    forward(2)
    arrived(abuf.at[:, x_cols], "A", 1)
    push(abuf.at[:, x_cols], abuf.at[:, x_cols], "A", r, base + sibling, 2)
    for k in range(1, Q):
        push(g_ref, gn.at[:, n_rows], "GN", r, base + node[k])
        push(d_ref.at[0], db.at[n_rows], "D", r, base + node[k])
    arrived(abuf.at[:, a_cols], "A", 0)
    arrived(abuf.at[:, a_cols], "A", 2)
    ah[...], al[...] = halves(abuf[...])
    product(0)
    product(1)
    relay(0)
    relay(1)

    def summed(j):
        arrived(rb.at[j], "RB", j)
        return ((pb[j, my_rows] + rb[j, 0]) + (rb[j, 1] + rb[j, 2])) + rb[j, 3]

    def to_unit(j, plane):
        @pl.when(z != plane)
        def _():
            push(yc.at[j], yu.at[my_rows], "YU", r, plane * Q + q, j)

        @pl.when(z == plane)
        def _():
            yu[my_rows] = yc[j]

    yc[0] = -weight(0, r) * summed(0)
    for k in range(1, Q):
        push(yc.at[0], y0n.at[:, n_cols], "Y0", r, base + node[k])
    for plane in planes[:3]:
        to_unit(0, plane)
    y0n[:, n_cols] = yc[0]
    product(2)
    arrived(y0n.at[:, : (Q - 1) * NQ], "Y0")
    out_ref[0] = y0n[n_rows]
    arrived(gc.at[:, : (R - 1) * HZ], "GP")
    for j in (1, 2):
        xc[j - 1] = mm(y0n[...], gc[j - 1])

    def child_columns(j):
        yc[j] = -weight(j, r) * (summed(j) + xc[j - 1])
        to_unit(j, planes[2 + j])
        for k in range(1, Q):
            push(
                yc.at[j, span(node[k], GC)], yo.at[j - 1, :, n_cols], "YO", r, base + node[k]
            )
        yo[j - 1, :, n_cols] = yc[j, n_rows]

    def rows_sum(unit, source, place):
        @pl.when(z == planes[unit])
        def _():
            arrived(yu.at[: (R - 1) * HZ], "YU", source)
            tp[...] = mm3(fh[...], fl[...], yu[...]).reshape(R, R, SP, NQ)
            zr[place, 0] = tp[z, r]

            for m in range(R):
                for k in range(R):
                    if m or k:
                        push(
                            tp.at[zs[m], rows[k]], zr.at[place, k], "ZM", rows[k], zc[m] + qs[k], place
                        )

    def cross_sum(unit, child):
        @pl.when(z == planes[unit])
        def _():
            arrived(yu.at[: (R - 1) * HZ], "YU", 0)
            y_hi, y_lo = halves(yu[...].T)
            total = dot(y_hi, fh[...]) + (dot(y_hi, fl[...]) + dot(y_lo, fh[...]))
            tpw[...] = (total * weight(1 + child, r)).reshape(HW, R, SP, W)

            for h in range(HW):
                dest = n * HW + h
                for k in range(R):
                    if k:
                        push(
                            tpw.at[h, rows[k]], wr.at[child, k], "WM", rows[k], dest * Q + qs[k], child
                        )
                        continue

                    @pl.when(dest == z)
                    def _():
                        wr[child, 0] = tpw[h, r]

                    @pl.when(dest != z)
                    def _():
                        push(tpw.at[h, r], wr.at[child, 0], "WM", r, dest * Q + q, child)

    def added(place, plane):
        @pl.when(z == plane)
        def _():
            arrived(zr.at[place, : R - 1], "ZM", place)

        @pl.when(z != plane)
        def _():
            arrived(zr.at[place], "ZM", place)

        return functools.reduce(jnp.add, [zr[place, k] for k in range(R)])

    relay(2)
    rows_sum(0, 0, 0)
    cross_sum(1, 0)
    cross_sum(2, 1)
    child_columns(1)
    child_columns(2)
    rows_sum(3, 1, 1)
    rows_sum(4, 2, 2)

    s_rows = span(r, SP)
    zm[...] = added(0, planes[0])
    for k in range(R):
        for w in range(Q):
            if k or w:
                push(zm, zb.at[s_rows, n_cols], "ZB", rows[k], base + node[w])

    zb[s_rows, n_cols] = zm[...]

    holds_w = lax.div(z, HW) == n

    @pl.when(holds_w)
    def _():
        for child in range(2):
            @pl.when(z == planes[1 + child])
            def _():
                arrived(wr.at[child, : R - 1], "WM", child)

            @pl.when(z != planes[1 + child])
            def _():
                arrived(wr.at[child], "WM", child)

            wm[child] = functools.reduce(jnp.add, [wr[child, k] for k in range(R)])

            for k in range(R):
                for w in range(Q):
                    if k or w:
                        share = (shares if k < HR else other_shares)[w]
                        push(
                            wm.at[child, :, span(share, NQ)], wb.at[child, s_rows], "WB",
                            rows[k], base + node[w], child,
                        )

            wb[child, s_rows] = wm[child, :, n_cols]

    loaded(dv, "LD")
    loaded(gn.at[:, n_rows], "LG")
    arrived(gn.at[:, : (Q - 1) * GC], "GN")
    arrived(db.at[: (Q - 1) * GC], "D")
    db[n_rows] = dv[0]
    arrived(fb.at[0, : (C - 1) * SP], "ZB")
    zb[...] = db[...] - zb[...]
    out_ref[3] = zb[n_rows]
    for child in range(2):
        @pl.when(holds_w)
        def _():
            arrived(wb.at[child, : (R - 1) * SP], "WB", child)

        @pl.when(jnp.logical_not(holds_w))
        def _():
            arrived(wb.at[child], "WB", child)

        eb[child] = wb[child] + mm(zb[...], gc[child])
        ge[child] = mm_t(gn[child], eb[child]).reshape(R, R, SP, NQ)
        for k in range(1, R):
            push(ge.at[child, zs[k], r], gz.at[child, R - 1 - k], "GZ", r, zc[k] + q, child)
        for k in range(1, Q):
            push(
                eb.at[child, span(node[k], GC)], uo.at[child, :, n_cols], "UO", r, base + node[k],
            )
        uo[child, :, n_cols] = eb[child, n_rows]

    o_place = lax.div(r, R // Q)
    o_rows = span(r - o_place * (R // Q), SP)
    for child in range(2):
        share = added(1 + child, planes[3 + child])
        arrived(gz.at[child], "GZ", child)
        total = ge[child, z, r] - share
        for k in range(R - 1):
            total = total + gz[child, k]
        zp[child] = total
        for k in range(1, R):
            push(
                zp.at[child], zo.at[child, o_rows, n_cols], "ZO", rows[k], base + o_place, child
            )

        @pl.when(q == o_place)
        def _():
            zo[child, o_rows, n_cols] = zp[child]

        @pl.when(q != o_place)
        def _():
            push(zp.at[child], zo.at[child, o_rows, n_cols], "ZO", r, base + o_place, child)

    arrived(yo.at[:, :, : (Q - 1) * NQ], "YO")
    out_ref[1:3] = yo[...]
    arrived(uo.at[:, :, : (Q - 1) * NQ], "UO")
    out_ref[6:8] = -uo[...]
    for child in range(2):
        @pl.when(q == o_place)
        def _():
            arrived(rb.at[child, 0, : (R - 1) * SP], "ZO", child)

        @pl.when(q != o_place)
        def _():
            arrived(rb.at[child, 0, : R * SP], "ZO", child)

        out_ref[4 + child] = dv[1 + child] + zo[child]

    for k in range(3):
        sent(abuf.at[:, a_cols], "A", k)
    sent(gc.at[:, : (Q - 1) * GC], "G0")
    sent(gc.at[:, : (R - 1) * HZ], "GP")
    sent(gn.at[:, : (Q - 1) * GC], "GN")
    sent(db.at[: (Q - 1) * GC], "D")
    sent(y0n.at[:, : (Q - 1) * NQ], "Y0")
    sent(yo.at[:, :, : (Q - 1) * NQ], "YO")
    sent(uo.at[:, :, : (Q - 1) * NQ], "UO")
    sent(fb.at[0, : (C - 1) * SP], "ZB")
    for j in range(3):
        @pl.when(near)
        def _():
            sent(fb.at[j], "FS", j)
            sent(fb.at[j, : (HR - 1) * HZ], "FA", j)

        @pl.when(r != z)
        def _():
            sent(fb.at[j, : (R - 2) * HZ], "FA", j)

        sent(xb.at[j], "X", j)
        sent(rb.at[j], "RB", j)

    @pl.when(r == partner)
    def _():
        sent(fb.at[:, : (HR - 1) * HZ], "FX")

    for j in range(3):
        targets = planes[:3] if j == 0 else planes[2 + j : 3 + j]
        inside = functools.reduce(jnp.logical_or, [z == plane for plane in targets])

        @pl.when(inside)
        def _():
            if len(targets) > 1:
                sent(yu.at[: (len(targets) - 1) * HZ], "YU", j)

        @pl.when(jnp.logical_not(inside))
        def _():
            sent(yu.at[: len(targets) * HZ], "YU", j)

    for unit, place in ((0, 0), (3, 1), (4, 2)):
        @pl.when(z == planes[unit])
        def _():
            sent(fb.at[0, : (R * R - 1) * SP], "ZM", place)

    for child in range(2):
        @pl.when((z == planes[1 + child]) & holds_w)
        def _():
            sent(fv.at[: (R * HW - 1) * SP], "WM", child)

        @pl.when((z == planes[1 + child]) & jnp.logical_not(holds_w))
        def _():
            sent(fv.at[: R * HW * SP], "WM", child)

    for child in range(2):
        @pl.when(holds_w)
        def _():
            sent(fb.at[0, : (C - 1) * SP], "WB", child)

        sent(gz.at[child], "GZ", child)

        @pl.when(q == o_place)
        def _():
            sent(rb.at[child, 0, : (R - 1) * SP], "ZO", child)

        @pl.when(q != o_place)
        def _():
            sent(rb.at[child, 0, : R * SP], "ZO", child)


def shards(region_inverse, factor_cols, parent_factor, diag_inverse, listed):
    R = lax.axis_size("row")
    C = lax.axis_size("col")
    W = factor_cols.shape[2]
    Q = C // R
    NQ, HZ, GC = W // Q, W // R, W // C
    SP = HZ // R
    HW = NQ // HZ
    planes = (0, 2, 5, 3, 7)
    f32 = jnp.float32
    vmem = pl.BlockSpec(memory_space=pltpu.VMEM)
    smem = pl.BlockSpec(memory_space=pltpu.SMEM)
    scratch = [
        (W, W), (3, W, NQ), (W, W), (3, W, NQ), (3, 3, HZ, NQ), (3, 2, HZ, NQ), (3, 4, HZ, NQ),
        (2, W, NQ), (2, HZ, W), (HZ, W), (3, GC, W), (HZ, W), (3, HZ, NQ), (2, HZ, NQ), (2, GC, W),
        (W, NQ), (R, R, SP, NQ), (HW, R, SP, W), (3, R, SP, NQ), (2, R, SP, W),
        (SP, NQ), (HZ, W), (2, SP, W), (2, HZ, NQ), (2, HZ, NQ), (2, GC, W),
        (2, R, R, SP, NQ), (2, R - 1, SP, NQ), (2, SP, NQ), (2, GC, W),
    ]
    hbm = pl.BlockSpec(memory_space=pl.ANY)
    whole = pl.pallas_call(
        functools.partial(kernel, R, C, W, planes),
        out_shape=jax.ShapeDtypeStruct((8, GC, W), f32),
        in_specs=[hbm, hbm, hbm, hbm, smem],
        out_specs=vmem,
        scratch_shapes=[pltpu.VMEM(shape, f32) for shape in scratch]
        + [pltpu.VMEM((W, W), jnp.bfloat16)] * 4
        + [pltpu.SemaphoreType.DMA((N_SEM,)), pltpu.SemaphoreType.DMA((N_SEM,))],
        compiler_params=pltpu.CompilerParams(
            collective_id=0, has_side_effects=True, vmem_limit_bytes=60 * 2**20
        ),
    )(region_inverse, factor_cols, parent_factor, diag_inverse, listed)
    return pl.pallas_call(
        split,
        out_shape=(
            jax.ShapeDtypeStruct((3, GC, W), f32),
            jax.ShapeDtypeStruct((3, GC, W), f32),
            jax.ShapeDtypeStruct((2, GC, W), f32),
        ),
        in_specs=[vmem],
        out_specs=(vmem, vmem, vmem),
        compiler_params=pltpu.CompilerParams(vmem_limit_bytes=4 * 2**20),
    )(whole)


def split(whole_ref, col_ref, diag_ref, par_ref):
    col_ref[...] = whole_ref[0:3]
    diag_ref[...] = whole_ref[3:6]
    par_ref[...] = whole_ref[6:8]


def solution(mesh):
    in_specs = (
        P("row", "col"),
        P(None, "row", None),
        P(None, "col", None),
        P(None, "col", None),
        P(),
    )
    out_specs = (P(None, ("row", "col"), None), P(None, "col", None), P(None, "col", None))
    return jax.shard_map(shards, mesh=mesh, in_specs=in_specs, out_specs=out_specs, check_vma=False)
```

```python
import functools

import jax
import jax.numpy as jnp
from jax import lax
from jax.experimental import pallas as pl
from jax.experimental.pallas import tpu as pltpu
from jax.sharding import PartitionSpec as P

MESH = pl.DeviceIdType.MESH
HIGH = lax.Precision.HIGHEST

SIZES = dict(
    A=3, FS=3, FA=3, FX=1, GN=1, G0=1, D=1, GP=1, X=3, RB=3, Y0=1, YO=1, YU=3, ZM=3, ZB=1, WM=2,
    WB=2, UO=1, GZ=2, ZO=2, FB=3, FV=1, LA=1, LG=1, LC=1, LD=1,
)
BASE = {}
N_SEM = 0
for _name, _size in SIZES.items():
    BASE[_name] = N_SEM
    N_SEM += _size

def halves(x):
    hi = x.astype(jnp.bfloat16)
    return hi, (x - hi.astype(jnp.float32)).astype(jnp.bfloat16)


def dot(a, b, dims=((1,), (0,))):
    return lax.dot_general(a, b, (dims, ((), ())), preferred_element_type=jnp.float32)


def mm3(a_hi, a_lo, b):
    b_hi, b_lo = halves(b)
    cols = b.shape[1]
    both = dot(a_hi, jnp.concatenate([b_hi, b_lo], axis=1))
    return both[:, :cols] + (both[:, cols:] + dot(a_lo, b_hi))


def mm(a, b):
    return mm3(*halves(a), b)


def mm_t(a, b):
    return lax.dot_general(
        a, b, (((0,), (0,)), ((), ())), precision=HIGH, preferred_element_type=jnp.float32
    )


def kernel(
    R, C, W, planes,
    a_ref, f_ref, g_ref, d_ref, listed_ref,
    out_ref,
    abuf, fb, fv, pb, xb, rl, rb, gc, gn, db, dv, y0n, yc, xc, yo, yu, tp, tpw, zr, wr,
    zm, zb, wm, wb, eb, uo, ge, gz, zp, zo, ah, al, fh, fl, send, recv,
):
    Q = C // R
    NQ, HZ, GC = W // Q, W // R, W // C
    SP = HZ // R
    HW = NQ // HZ
    HR = R // 2
    r = lax.axis_index("row")
    c = lax.axis_index("col")

    def wrap(value, size):
        return jnp.where(value >= size, value - size, value)

    z = lax.div(c, Q)
    q = c - z * Q
    half = lax.div(r, HR)
    y = r - half * HR
    pair = lax.div(q, 2)
    core = q - pair * 2
    z_half = lax.div(z, HR)
    kind = jnp.where(pair == half, 0, 1)
    across = 2 * (1 - pair) + core
    sibling = 2 * pair + 1 - core
    diagonal = 2 * (1 - pair) + 1 - core
    node = (q, sibling, across, diagonal)
    n = 2 * kind + core
    shares = (n, 2 * kind + 1 - core, 2 * (1 - kind) + core, 2 * (1 - kind) + 1 - core)
    other_shares = (shares[2], shares[3], shares[0], shares[1])
    ys = [wrap(y + k, HR) if k else y for k in range(HR)]
    rows = [half * HR + v for v in ys] + [(1 - half) * HR + v for v in ys]
    qs = [q] * HR + [across] * HR
    zs = [wrap(z + k, R) if k else z for k in range(R)]
    zc = [v * Q for v in zs]
    base = zc[0]
    zd = [zs[k] if k % HR == 0 else jnp.where(core == 0, zs[k], zs[R - k]) for k in range(R)]
    partner = z + HR - 2 * HR * z_half

    def span(i, size):
        return pl.ds(pl.multiple_of(i * size, size), size)

    def piece(i):
        return span(i, HZ)

    n_cols = span(n, NQ)
    my_rows = piece(z)

    def push(src, dst, s, row, col, k=0):
        s = BASE[s] + k
        pltpu.make_async_remote_copy(
            src_ref=src, dst_ref=dst, send_sem=send.at[s], recv_sem=recv.at[s],
            device_id=(row, col), device_id_type=MESH,
        ).start()

    def arrived(view, s, k=0):
        pltpu.make_async_copy(view, view, recv.at[BASE[s] + k]).wait()

    def sent(view, s, k=0):
        pltpu.make_async_copy(view, view, send.at[BASE[s] + k]).wait()

    def weight(member, block):
        return listed_ref[member, block].astype(jnp.float32)

    barrier = pltpu.get_barrier_semaphore()

    def greet(row, col):
        pl.semaphore_signal(barrier, inc=1, device_id=(row, col), device_id_type=MESH)

    for k in range(1, R):
        greet(rows[k], base + qs[k])
    for k in range(1, R):
        greet(r, zc[k] + q)
    for k in range(1, Q):
        greet(r, base + node[k])
    near = z == r
    a_cols = span(q, NQ)
    x_cols = span(across, NQ)
    n_rows = span(q, GC)
    g_rows = span(c, GC)

    def local(src, dst, s, k=0):
        pltpu.make_async_copy(src, dst, recv.at[BASE[s] + k]).start()

    def loaded(view, s, k=0):
        pltpu.make_async_copy(view, view, recv.at[BASE[s] + k]).wait()

    @pl.when(near)
    def _():
        for j in range(3):
            local(f_ref.at[j, :, n_cols], fb.at[j], "FB", j)

    local(a_ref, abuf.at[:, a_cols], "LA")
    local(g_ref.at[:, :, n_cols], gc.at[:, g_rows], "LC")
    for unit, member in enumerate((0, 1, 2, 1, 2)):
        @pl.when(z == planes[unit])
        def _():
            local(f_ref.at[member], fv, "FV")


    local(g_ref, gn.at[:, n_rows], "LG")
    local(d_ref, dv, "LD")
    in_cols = functools.reduce(jnp.logical_or, [z == planes[unit] for unit in (0, 3, 4)])
    in_rows = functools.reduce(jnp.logical_or, [z == planes[unit] for unit in (1, 2)])

    @pl.when(in_cols)
    def _():
        loaded(fv, "FV")
        fh[...], fl[...] = halves(fv[...].T)

    @pl.when(in_rows)
    def _():
        loaded(fv, "FV")
        fh[...], fl[...] = halves(fv[...])

    pl.semaphore_wait(barrier, 2 * (R - 1) + Q - 1)

    @pl.when(near)
    def _():
        for j in range(3):
            loaded(fb.at[j], "FB", j)
            for k in range(1, R):
                push(
                    fb.at[j, piece(rows[k])], fb.at[j, piece(rows[k])], "FS", rows[k], base + qs[k], j
                )
            push(fb.at[j, piece(z)], fb.at[j, piece(z)], "FS", rows[HR], base + across, j)
            for k in range(1, HR):
                push(fb.at[j, piece(z)], fb.at[j, piece(z)], "FA", rows[k], base + q, j)

    for k in range(1, Q):
        push(g_ref.at[:, :, span(shares[k], NQ)], gc.at[:, g_rows], "G0", r, base + node[k])
    loaded(abuf.at[:, a_cols], "LA")
    push(abuf.at[:, a_cols], abuf.at[:, a_cols], "A", r, base + across, 1)
    push(abuf.at[:, a_cols], abuf.at[:, a_cols], "A", r, base + sibling, 0)

    def forward(j):
        @pl.when(r != z)
        def _():
            @pl.when(r == partner)
            def _():
                arrived(fb.at[j, : 2 * HZ], "FS", j)

            @pl.when(r != partner)
            def _():
                arrived(fb.at[j, :HZ], "FS", j)

            for k in range(1, R):
                @pl.when(rows[k] != z)
                def _():
                    push(fb.at[j, piece(r)], fb.at[j, piece(r)], "FA", rows[k], base + qs[k], j)

            @pl.when(r == partner)
            def _():
                for k in range(1, HR):
                    pltpu.make_async_remote_copy(
                        src_ref=fb.at[j, piece(z)], dst_ref=fb.at[j, piece(z)],
                        send_sem=send.at[BASE["FX"]], recv_sem=recv.at[BASE["FA"] + j],
                        device_id=(rows[k], base + q), device_id_type=MESH,
                    ).start()

    def share_columns():
        loaded(gc.at[:, g_rows], "LC")
        arrived(gc.at[:, : (Q - 1) * GC], "G0")
        for k in range(1, R):
            push(gc.at[:, my_rows], gc.at[:, my_rows], "GP", r, zc[k] + q)

    def along(k):
        return zd[k % R]

    def product(j):
        @pl.when((r != z) & (r != partner))
        def _():
            arrived(fb.at[j, : (R - 1) * HZ], "FA", j)

        @pl.when(r == partner)
        def _():
            arrived(fb.at[j, : (R - 2) * HZ], "FA", j)

        pb[j] = mm3(ah[...], al[...], fb[j]) * weight(j, z)

        def part(k):
            return pb.at[j, piece(along(k))]

        push(part(4), xb.at[j, 0], "X", r, along(2) * Q + q, j)
        push(part(3), xb.at[j, 1], "X", r, along(1) * Q + q, j)
        push(part(-3), xb.at[j, 2], "X", r, along(-1) * Q + q, j)
        push(part(1), rb.at[j, 0], "RB", r, along(1) * Q + q, j)
        push(part(-1), rb.at[j, 1], "RB", r, along(-1) * Q + q, j)

    def relay(j):
        arrived(xb.at[j], "X", j)
        rl[j, 0] = pb[j, piece(along(2))] + xb[j, 0] + xb[j, 1]
        rl[j, 1] = pb[j, piece(along(-2))] + xb[j, 2]
        push(rl.at[j, 0], rb.at[j, 2], "RB", r, along(2) * Q + q, j)
        push(rl.at[j, 1], rb.at[j, 3], "RB", r, along(-2) * Q + q, j)

    share_columns()
    forward(0)
    forward(1)
    forward(2)
    arrived(abuf.at[:, x_cols], "A", 1)
    push(abuf.at[:, x_cols], abuf.at[:, x_cols], "A", r, base + sibling, 2)
    for k in range(1, Q):
        push(g_ref, gn.at[:, n_rows], "GN", r, base + node[k])
        push(d_ref.at[0], db.at[n_rows], "D", r, base + node[k])
    arrived(abuf.at[:, a_cols], "A", 0)
    arrived(abuf.at[:, a_cols], "A", 2)
    ah[...], al[...] = halves(abuf[...])
    product(0)
    product(1)
    relay(0)
    relay(1)

    def summed(j):
        arrived(rb.at[j], "RB", j)
        return ((pb[j, my_rows] + rb[j, 0]) + (rb[j, 1] + rb[j, 2])) + rb[j, 3]

    def to_unit(j, plane):
        @pl.when(z != plane)
        def _():
            push(yc.at[j], yu.at[my_rows], "YU", r, plane * Q + q, j)

        @pl.when(z == plane)
        def _():
            yu[my_rows] = yc[j]

    yc[0] = -weight(0, r) * summed(0)
    for k in range(1, Q):
        push(yc.at[0], y0n.at[:, n_cols], "Y0", r, base + node[k])
    for plane in planes[:3]:
        to_unit(0, plane)
    y0n[:, n_cols] = yc[0]
    product(2)
    arrived(y0n.at[:, : (Q - 1) * NQ], "Y0")
    out_ref[0] = y0n[n_rows]
    arrived(gc.at[:, : (R - 1) * HZ], "GP")
    for j in (1, 2):
        xc[j - 1] = mm(y0n[...], gc[j - 1])

    def child_columns(j):
        yc[j] = -weight(j, r) * (summed(j) + xc[j - 1])
        to_unit(j, planes[2 + j])
        for k in range(1, Q):
            push(
                yc.at[j, span(node[k], GC)], yo.at[j - 1, :, n_cols], "YO", r, base + node[k]
            )
        yo[j - 1, :, n_cols] = yc[j, n_rows]

    def rows_sum(unit, source, place):
        @pl.when(z == planes[unit])
        def _():
            arrived(yu.at[: (R - 1) * HZ], "YU", source)
            tp[...] = mm3(fh[...], fl[...], yu[...]).reshape(R, R, SP, NQ)
            zr[place, 0] = tp[z, r]

            for m in range(R):
                for k in range(R):
                    if m or k:
                        push(
                            tp.at[zs[m], rows[k]], zr.at[place, k], "ZM", rows[k], zc[m] + qs[k], place
                        )

    def cross_sum(unit, child):
        @pl.when(z == planes[unit])
        def _():
            arrived(yu.at[: (R - 1) * HZ], "YU", 0)
            y_hi, y_lo = halves(yu[...].T)
            total = dot(y_hi, fh[...]) + (dot(y_hi, fl[...]) + dot(y_lo, fh[...]))
            tpw[...] = (total * weight(1 + child, r)).reshape(HW, R, SP, W)

            for h in range(HW):
                dest = n * HW + h
                for k in range(R):
                    if k:
                        push(
                            tpw.at[h, rows[k]], wr.at[child, k], "WM", rows[k], dest * Q + qs[k], child
                        )
                        continue

                    @pl.when(dest == z)
                    def _():
                        wr[child, 0] = tpw[h, r]

                    @pl.when(dest != z)
                    def _():
                        push(tpw.at[h, r], wr.at[child, 0], "WM", r, dest * Q + q, child)

    def added(place, plane):
        @pl.when(z == plane)
        def _():
            arrived(zr.at[place, : R - 1], "ZM", place)

        @pl.when(z != plane)
        def _():
            arrived(zr.at[place], "ZM", place)

        return functools.reduce(jnp.add, [zr[place, k] for k in range(R)])

    relay(2)
    rows_sum(0, 0, 0)
    cross_sum(1, 0)
    cross_sum(2, 1)
    child_columns(1)
    child_columns(2)
    rows_sum(3, 1, 1)
    rows_sum(4, 2, 2)

    s_rows = span(r, SP)
    zm[...] = added(0, planes[0])
    for k in range(R):
        for w in range(Q):
            if k or w:
                push(zm, zb.at[s_rows, n_cols], "ZB", rows[k], base + node[w])

    zb[s_rows, n_cols] = zm[...]

    holds_w = lax.div(z, HW) == n

    @pl.when(holds_w)
    def _():
        for child in range(2):
            @pl.when(z == planes[1 + child])
            def _():
                arrived(wr.at[child, : R - 1], "WM", child)

            @pl.when(z != planes[1 + child])
            def _():
                arrived(wr.at[child], "WM", child)

            wm[child] = functools.reduce(jnp.add, [wr[child, k] for k in range(R)])

            for k in range(R):
                for w in range(Q):
                    if k or w:
                        share = (shares if k < HR else other_shares)[w]
                        push(
                            wm.at[child, :, span(share, NQ)], wb.at[child, s_rows], "WB",
                            rows[k], base + node[w], child,
                        )

            wb[child, s_rows] = wm[child, :, n_cols]

    loaded(dv, "LD")
    loaded(gn.at[:, n_rows], "LG")
    arrived(gn.at[:, : (Q - 1) * GC], "GN")
    arrived(db.at[: (Q - 1) * GC], "D")
    db[n_rows] = dv[0]
    arrived(fb.at[0, : (C - 1) * SP], "ZB")
    zb[...] = db[...] - zb[...]
    out_ref[3] = zb[n_rows]
    for child in range(2):
        @pl.when(holds_w)
        def _():
            arrived(wb.at[child, : (R - 1) * SP], "WB", child)

        @pl.when(jnp.logical_not(holds_w))
        def _():
            arrived(wb.at[child], "WB", child)

        eb[child] = wb[child] + mm(zb[...], gc[child])
        ge[child] = mm_t(gn[child], eb[child]).reshape(R, R, SP, NQ)
        for k in range(1, R):
            push(ge.at[child, zs[k], r], gz.at[child, R - 1 - k], "GZ", r, zc[k] + q, child)
        for k in range(1, Q):
            push(
                eb.at[child, span(node[k], GC)], uo.at[child, :, n_cols], "UO", r, base + node[k],
            )
        uo[child, :, n_cols] = eb[child, n_rows]

    o_place = lax.div(r, R // Q)
    o_rows = span(r - o_place * (R // Q), SP)
    for child in range(2):
        share = added(1 + child, planes[3 + child])
        arrived(gz.at[child], "GZ", child)
        total = ge[child, z, r] - share
        for k in range(R - 1):
            total = total + gz[child, k]
        zp[child] = total
        for k in range(1, R):
            push(
                zp.at[child], zo.at[child, o_rows, n_cols], "ZO", rows[k], base + o_place, child
            )

        @pl.when(q == o_place)
        def _():
            zo[child, o_rows, n_cols] = zp[child]

        @pl.when(q != o_place)
        def _():
            push(zp.at[child], zo.at[child, o_rows, n_cols], "ZO", r, base + o_place, child)

    arrived(yo.at[:, :, : (Q - 1) * NQ], "YO")
    out_ref[1:3] = yo[...]
    arrived(uo.at[:, :, : (Q - 1) * NQ], "UO")
    out_ref[6:8] = -uo[...]
    for child in range(2):
        @pl.when(q == o_place)
        def _():
            arrived(rb.at[child, 0, : (R - 1) * SP], "ZO", child)

        @pl.when(q != o_place)
        def _():
            arrived(rb.at[child, 0, : R * SP], "ZO", child)

        out_ref[4 + child] = dv[1 + child] + zo[child]

    for k in range(3):
        sent(abuf.at[:, a_cols], "A", k)
    sent(gc.at[:, : (Q - 1) * GC], "G0")
    sent(gc.at[:, : (R - 1) * HZ], "GP")
    sent(gn.at[:, : (Q - 1) * GC], "GN")
    sent(db.at[: (Q - 1) * GC], "D")
    sent(y0n.at[:, : (Q - 1) * NQ], "Y0")
    sent(yo.at[:, :, : (Q - 1) * NQ], "YO")
    sent(uo.at[:, :, : (Q - 1) * NQ], "UO")
    sent(fb.at[0, : (C - 1) * SP], "ZB")
    for j in range(3):
        @pl.when(near)
        def _():
            sent(fb.at[j], "FS", j)
            sent(fb.at[j, : (HR - 1) * HZ], "FA", j)

        @pl.when(r != z)
        def _():
            sent(fb.at[j, : (R - 2) * HZ], "FA", j)

        sent(xb.at[j], "X", j)
        sent(rb.at[j], "RB", j)

    @pl.when(r == partner)
    def _():
        sent(fb.at[:, : (HR - 1) * HZ], "FX")

    for j in range(3):
        targets = planes[:3] if j == 0 else planes[2 + j : 3 + j]
        inside = functools.reduce(jnp.logical_or, [z == plane for plane in targets])

        @pl.when(inside)
        def _():
            if len(targets) > 1:
                sent(yu.at[: (len(targets) - 1) * HZ], "YU", j)

        @pl.when(jnp.logical_not(inside))
        def _():
            sent(yu.at[: len(targets) * HZ], "YU", j)

    for unit, place in ((0, 0), (3, 1), (4, 2)):
        @pl.when(z == planes[unit])
        def _():
            sent(fb.at[0, : (R * R - 1) * SP], "ZM", place)

    for child in range(2):
        @pl.when((z == planes[1 + child]) & holds_w)
        def _():
            sent(fv.at[: (R * HW - 1) * SP], "WM", child)

        @pl.when((z == planes[1 + child]) & jnp.logical_not(holds_w))
        def _():
            sent(fv.at[: R * HW * SP], "WM", child)

    for child in range(2):
        @pl.when(holds_w)
        def _():
            sent(fb.at[0, : (C - 1) * SP], "WB", child)

        sent(gz.at[child], "GZ", child)

        @pl.when(q == o_place)
        def _():
            sent(rb.at[child, 0, : (R - 1) * SP], "ZO", child)

        @pl.when(q != o_place)
        def _():
            sent(rb.at[child, 0, : R * SP], "ZO", child)


def shards(region_inverse, factor_cols, parent_factor, diag_inverse, listed):
    R = lax.axis_size("row")
    C = lax.axis_size("col")
    W = factor_cols.shape[2]
    Q = C // R
    NQ, HZ, GC = W // Q, W // R, W // C
    SP = HZ // R
    HW = NQ // HZ
    planes = (0, 2, 5, 3, 7)
    f32 = jnp.float32
    vmem = pl.BlockSpec(memory_space=pltpu.VMEM)
    smem = pl.BlockSpec(memory_space=pltpu.SMEM)
    scratch = [
        (W, W), (3, W, NQ), (W, W), (3, W, NQ), (3, 3, HZ, NQ), (3, 2, HZ, NQ), (3, 4, HZ, NQ),
        (2, W, NQ), (2, HZ, W), (HZ, W), (3, GC, W), (HZ, W), (3, HZ, NQ), (2, HZ, NQ), (2, GC, W),
        (W, NQ), (R, R, SP, NQ), (HW, R, SP, W), (3, R, SP, NQ), (2, R, SP, W),
        (SP, NQ), (HZ, W), (2, SP, W), (2, HZ, NQ), (2, HZ, NQ), (2, GC, W),
        (2, R, R, SP, NQ), (2, R - 1, SP, NQ), (2, SP, NQ), (2, GC, W),
    ]
    hbm = pl.BlockSpec(memory_space=pl.ANY)
    whole = pl.pallas_call(
        functools.partial(kernel, R, C, W, planes),
        out_shape=jax.ShapeDtypeStruct((8, GC, W), f32),
        in_specs=[hbm, hbm, hbm, hbm, smem],
        out_specs=vmem,
        scratch_shapes=[pltpu.VMEM(shape, f32) for shape in scratch]
        + [pltpu.VMEM((W, W), jnp.bfloat16)] * 4
        + [pltpu.SemaphoreType.DMA((N_SEM,)), pltpu.SemaphoreType.DMA((N_SEM,))],
        compiler_params=pltpu.CompilerParams(
            collective_id=0, has_side_effects=True, vmem_limit_bytes=60 * 2**20
        ),
    )(region_inverse, factor_cols, parent_factor, diag_inverse, listed)
    return pl.pallas_call(
        split,
        out_shape=(
            jax.ShapeDtypeStruct((3, GC, W), f32),
            jax.ShapeDtypeStruct((3, GC, W), f32),
            jax.ShapeDtypeStruct((2, GC, W), f32),
        ),
        in_specs=[hbm],
        out_specs=(vmem, vmem, vmem),
        scratch_shapes=[pltpu.SemaphoreType.DMA((3,))],
        compiler_params=pltpu.CompilerParams(vmem_limit_bytes=60 * 2**20),
    )(whole)


def split(whole_ref, col_ref, diag_ref, par_ref, sems):
    parts = ((0, 3, col_ref), (3, 6, diag_ref), (6, 8, par_ref))
    copies = [
        pltpu.make_async_copy(whole_ref.at[first:last], ref, sems.at[k])
        for k, (first, last, ref) in enumerate(parts)
    ]
    for copy in copies:
        copy.start()
    for copy in copies:
        copy.wait()


def solution(mesh):
    in_specs = (
        P("row", "col"),
        P(None, "row", None),
        P(None, "col", None),
        P(None, "col", None),
        P(),
    )
    out_specs = (P(None, ("row", "col"), None), P(None, "col", None), P(None, "col", None))
    return jax.shard_map(shards, mesh=mesh, in_specs=in_specs, out_specs=out_specs, check_vma=False)
```
